32 devices in a mesh: gx: 8 (over y, x, core), yz: 4 (over z).
Axes of the slice: x: 2, y: 2, z: 4, core: 2. Of those that a mesh axis runs over, the one named last changes fastest.
Arguments:
- residual: float32 [96, 8, 64, 128], P('gx', 'yz'), may hold values from -0.3 to 0.3
- inverses: float32 [96, 8, 64, 64], P('gx', 'yz'), may hold values from -0.25 to 1
- upwind: float32 [8, 64, 64], replicated, may hold values from -0.25 to 1
- downwind: float32 [8, 64, 64], replicated, may hold values from -0.25 to 1
- flux_y: float32 [8, 64, 64], replicated, may hold values from -0.75 to 0.75
- kinds: int32 [8], P('yz'), may hold values from 0 to 7
- volume_category: int32 [96, 8, 128], P('gx', 'yz'), may hold values from 0 to 2, as said below
Outputs:
- adjoint: float32 [96, 8, 64, 128], P('gx', 'yz')
The draws below stay inside these ranges and needn't reach their ends.
Inputs may be any that keep to these rules, and one draw needn't show every extreme that they name: `volume_category`: 0 marks a fluid cell, 1 a wall cell, 2 an inflow cell.
All inputs are finite; a program needn't handle non-finite values.
Results may differ from the reference program's by a relative error of at most 0.00026.
Values sent between devices are 32-bit elements; how exact they have to be, the bound alone decides.
A program may use at most 64 MiB of HBM per device.

```python
import math
import jax
import jax.numpy as jnp
from jax import lax

NV = 64
NK = 8
NZ = 128
CELLS_PER_XLINE = 96
LINE_GROUP_TOTAL = 8


def rotation(key, lead, strength):
    noise = jax.random.normal(key, lead + (NV, NV), jnp.float32)
    skew_part = strength * 0.5 * (noise - jnp.swapaxes(noise, -1, -2))
    identity = jnp.broadcast_to(jnp.eye(NV, dtype=jnp.float32), lead + (NV, NV))
    term = identity
    total = identity
    for order in range(1, 11):
        term = jnp.matmul(term, skew_part, precision=lax.Precision.HIGHEST) / float(order)
        total = total + term
    return total


def draw_inverses(key, part):
    key_seed_root, key_jagged_draw, key_pulse_draw, key_blend_draw = jax.random.split(key, 4)
    magnitude_multipliers = jnp.exp(jax.random.uniform(key_seed_root, (1, LINE_GROUP_TOTAL, NV, 1), jnp.float32, math.log(0.993), math.log(0.999)))
    irregular_profile = jax.random.uniform(key_jagged_draw, (CELLS_PER_XLINE, LINE_GROUP_TOTAL, NV, 1), jnp.float32, 0.996, 1.0)
    selected_items = jax.random.randint(key_pulse_draw, (CELLS_PER_XLINE, LINE_GROUP_TOTAL, 1, 1), 0, 256)
    sudden_impulses = jnp.where(selected_items == 0, 0.85, 1.0).astype(jnp.float32)

    def one_plane(index):
        return rotation(jax.random.fold_in(key_blend_draw, index), (LINE_GROUP_TOTAL,), 0.04)
    mixing_weights = lax.map(one_plane, jnp.arange(CELLS_PER_XLINE, dtype=jnp.int32))
    return magnitude_multipliers * irregular_profile * sudden_impulses * mixing_weights


def transport_table(key, salt):
    key_scale, key_blend_draw = jax.random.split(jax.random.fold_in(key, salt))
    magnitude_multipliers = jax.random.uniform(key_scale, (NK, NV, 1), jnp.float32, 0.997, 1.0)
    return magnitude_multipliers * rotation(key_blend_draw, (NK,), 0.04)


def draw_upwind(key, part):
    return transport_table(key, 11)


def draw_downwind(key, part):
    return transport_table(key, 23)


def draw_volume_category(key, part):
    selected_items = jax.random.randint(key, (CELLS_PER_XLINE, LINE_GROUP_TOTAL, NZ), 0, 8)
    return jnp.where(selected_items == 0, 1, jnp.where(selected_items == 1, 2, 0)).astype(jnp.int32)


def plant(entries, key, least, high):
    spot = [jax.random.randint(jax.random.fold_in(key, axis), (), 0, length) for axis, length in enumerate(entries.shape)]
    longest = entries.shape.index(max(entries.shape))
    next_to = spot[:longest] + [(spot[longest] + 1) % entries.shape[longest]] + spot[longest + 1:]
    return entries.at[tuple(spot)].set(least).at[tuple(next_to)].set(high)


def block_scale(own_key, extent, shards, least, top_value):
    factor_of = 1.0
    for axis_at, shards_of in shards:
        draws = jax.random.uniform(jax.random.fold_in(jax.random.fold_in(own_key, 6), axis_at), (shards_of,), jnp.float32, least / len(shards), top_value / len(shards))
        factor_of = factor_of * jnp.repeat(jnp.exp(draws), extent[axis_at] // shards_of).reshape((-1,) + (1,) * (len(extent) - 1 - axis_at))
    return factor_of


def gaussian(own_key, extent, deviation, bound, pieces=(), kind=jnp.bfloat16):
    drawn = deviation * jax.random.normal(own_key, extent, jnp.float32)
    if pieces:
        drawn = drawn * block_scale(own_key, extent, pieces, -0.22, 0.18)
    return jnp.clip(drawn, -bound, bound).astype(kind)


def setup_inputs(seed: int = 0) -> dict:
    key_list = jax.random.split(jax.random.key(seed), 8)
    residual = gaussian(key_list[0], (CELLS_PER_XLINE, LINE_GROUP_TOTAL, NV, NZ), 0.05, 0.3, ((0, 8), (1, 4)), jnp.float32)
    inverses = draw_inverses(jax.random.fold_in(key_list[7], 71), 0)
    upwind = draw_upwind(jax.random.fold_in(key_list[7], 71), 0)
    downwind = draw_downwind(jax.random.fold_in(key_list[7], 71), 0)
    flux_y = gaussian(key_list[4], (NK, NV, NV), NV ** -0.5, 0.75, (), jnp.float32)
    kinds = plant(jax.random.randint(key_list[5], (LINE_GROUP_TOTAL,), 0, NK), jax.random.fold_in(key_list[5], 1), 0, NK - 1).astype(jnp.int32)
    volume_category = draw_volume_category(jax.random.fold_in(key_list[7], 71), 0)
    return dict(residual=residual, inverses=inverses, upwind=upwind, downwind=downwind, flux_y=flux_y, kinds=kinds, volume_category=volume_category)


HIGHEST = lax.Precision.HIGHEST


def apply_transposed(matrices, vectors):
    return jnp.einsum("gab,gaz->gbz", matrices, vectors, precision=HIGHEST)


def select_rows(kinds, table):
    kind_count = table.shape[0]
    one_hot = (kinds[:, None] == jnp.arange(kind_count, dtype=jnp.int32)[None, :]).astype(jnp.float32)
    flat = jnp.dot(one_hot, table.reshape(kind_count, -1), precision=HIGHEST, preferred_element_type=jnp.float32)
    return flat.reshape(kinds.shape[0], table.shape[1], table.shape[2])


def source_weight(volume_category):
    fluid = (volume_category == 0).astype(jnp.float32)
    inflow = (volume_category == 2).astype(jnp.float32)
    return (fluid + 0.5 * inflow)[:, :, None, :]


def y_derivative(padded):
    return (8.0 * (padded[:, 3:-1] - padded[:, 1:-3]) - (padded[:, 4:] - padded[:, :-4])) / 12.0


def reference(residual, inverses, upwind, downwind, flux_y, kinds, volume_category):
    up_rows = select_rows(kinds, upwind)
    lower_neighbors = select_rows(kinds, downwind)
    flux_rows = select_rows(kinds, flux_y)
    padded = jnp.pad(residual, ((0, 0), (2, 2), (0, 0), (0, 0)))
    derivative = y_derivative(padded)
    flux = jnp.einsum("yab,xyaz->xybz", flux_rows, derivative, precision=HIGHEST)
    forcing = source_weight(volume_category) * (residual + flux)

    def forward_step(carried, cell_data):
        forcing_cell, inverse_cell = cell_data
        eliminated = forcing_cell - apply_transposed(up_rows, carried)
        return apply_transposed(inverse_cell, eliminated), eliminated

    initial = jnp.zeros((residual.shape[1], residual.shape[2], residual.shape[3]), jnp.float32)
    last_value, eliminated = lax.scan(forward_step, initial, (forcing, inverses))

    def backward_step(carried, cell_data):
        eliminated_cell, inverse_cell = cell_data
        updated = apply_transposed(inverse_cell, eliminated_cell - apply_transposed(lower_neighbors, carried))
        return updated, updated

    first_value, adjoint = lax.scan(backward_step, initial, (eliminated, inverses), reverse=True)
    wet_cells = (volume_category != 1).astype(jnp.float32)[:, :, None, :]
    return adjoint * wet_cells
```

```python
import functools

import jax
import jax.numpy as jnp
from jax import lax
from jax.experimental import pallas as pl
from jax.experimental.pallas import tpu as pltpu
from jax.sharding import PartitionSpec as P

MESH = pl.DeviceIdType.MESH
F32 = jnp.float32
BF16 = jnp.bfloat16


def split(a):
    high = a.astype(BF16)
    return high, (a - high.astype(F32)).astype(BF16)


def mul(a, b):
    ah, al = a
    bh, bl = b
    d = functools.partial(jnp.dot, preferred_element_type=F32)
    return d(ah, bh) + (d(ah, bl) + d(al, bh))


def loop(count, body, carry, unroll=1):
    unroll = unroll if count % unroll == 0 else 1

    def several(i, carry):
        for u in range(unroll):
            carry = body(i * unroll + u, carry)
        return carry

    return lax.fori_loop(0, count // unroll, several, carry)


def kernel(
    n_gx, n_yz, chunk, res_hbm, inv_hbm, up_hbm, down_hbm, flux_hbm, cat_hbm, kinds_hbm, out,
    res, inv, up, down, flux, cat, kinds,
    snd, low, high, table, vt, ft, bt, hom, omega, gain, fast, resp, cs, acc, gmap, given, taken,
    send_map, ahead, behind, mirror, wide_state, tall, into_state,
    load_sem, halo_send, halo_recv, map_send, map_recv, vec_send, vec_recv,
):
    cells, groups, nv, nz = res.shape
    half = n_gx // 2
    pieces = cells // chunk
    gx = lax.axis_index("gx")
    yz = lax.axis_index("yz")
    partner = gx + 1 - 2 * lax.rem(gx, 2)
    has_low = yz > 0
    has_high = yz < n_yz - 1

    loads = [
        pltpu.make_async_copy(source, target, load_sem.at[n])
        for n, (source, target) in enumerate(
            (
                (res_hbm, res), (inv_hbm, inv), (up_hbm, up), (down_hbm, down),
                (flux_hbm, flux), (cat_hbm, cat), (kinds_hbm, kinds),
            )
        )
    ]
    for load in loads:
        load.start()

    def peer(k):
        return lax.rem(gx + 2 * k, n_gx)

    barrier = pltpu.get_barrier_semaphore()
    for k in range(1, n_gx):
        pl.semaphore_signal(
            barrier, inc=1, device_id=(lax.rem(gx + k, n_gx), yz), device_id_type=MESH
        )

    @pl.when(has_low)
    def _():
        pl.semaphore_signal(barrier, inc=1, device_id=(gx, yz - 1), device_id_type=MESH)

    @pl.when(has_high)
    def _():
        pl.semaphore_signal(barrier, inc=1, device_id=(gx, yz + 1), device_id_type=MESH)

    pl.semaphore_wait(barrier, n_gx - 1 + jnp.where(has_low, 1, 0) + jnp.where(has_high, 1, 0))

    def halo(direction, g, c):
        part = pl.ds(c * chunk, chunk)
        if direction == 0:
            src = snd.at[0, part] if g == 0 else res_hbm.at[part, 1]
            dst, where = low, yz + 1
        else:
            src = res_hbm.at[part, 0] if g == 0 else snd.at[1, part]
            dst, where = high, yz - 1
        return pltpu.make_async_remote_copy(
            src_ref=src,
            dst_ref=dst.at[g, part],
            send_sem=halo_send.at[direction, g, c],
            recv_sem=halo_recv.at[direction, g, c],
            device_id=(gx, where),
            device_id_type=MESH,
        )

    @pl.when(has_low)
    def _():
        for c in range(pieces):
            halo(1, 0, c).start()

    loads[0].wait()

    for c in range(pieces):
        for x in range(c * chunk, (c + 1) * chunk):
            snd[0, x] = res[x, 0] - 8.0 * res[x, 1]

        @pl.when(has_high)
        def _():
            halo(0, 0, c).start()

    @pl.when(has_high)
    def _():
        for c in range(pieces):
            halo(0, 1, c).start()

    for c in range(pieces):
        for x in range(c * chunk, (c + 1) * chunk):
            snd[1, x] = 8.0 * res[x, 0] - res[x, 1]

        @pl.when(has_low)
        def _():
            halo(1, 1, c).start()

    @pl.when(jnp.logical_not(has_low))
    def _():
        low[...] = jnp.zeros_like(low)

    @pl.when(jnp.logical_not(has_high))
    def _():
        high[...] = jnp.zeros_like(high)

    for load in loads[1:]:
        load.wait()

    for g in range(groups):
        kind = kinds[g]
        for n, block in enumerate((flux[kind] * (1.0 / 12.0), -up[kind], -down[kind])):
            table[g, n, 0], table[g, n, 1] = split(block.T)

    def held(g, n):
        return table[g, n, 0], table[g, n, 1]

    def put(ref, g, x, pair):
        ref[g, x, 0], ref[g, x, 1] = pair

    def get(ref, g, x):
        return ref[g, x, 0], ref[g, x, 1]

    def steps(x, carry):
        for g in range(groups):
            v = split(inv[x, g].T)
            put(vt, g, x, v)
            put(ft, g, x, split(mul(v, held(g, 1))))
            put(bt, g, x, split(mul(v, held(g, 2))))
        return carry

    loop(cells, steps, 0, 4)

    row = lax.broadcasted_iota(jnp.int32, (nv, 2 * nv), 0)
    col = lax.broadcasted_iota(jnp.int32, (nv, 2 * nv), 1)
    first_unit = (row == col).astype(F32)
    second_unit = (row + nv == col).astype(F32)
    square_row = lax.broadcasted_iota(jnp.int32, (nv, nv), 0)
    square_col = lax.broadcasted_iota(jnp.int32, (nv, nv), 1)
    unit = (square_row == square_col).astype(F32)
    for g in range(groups):
        hom[g, 0] = first_unit
        omega[g, 0] = unit

    def hom_forward(x, carry):
        for g in range(groups):
            hom[g, x + 1] = mul(get(ft, g, x), split(hom[g, x]))
            omega[g, x + 1] = mul(split(omega[g, x]), get(bt, g, x))
        return carry

    loop(cells, hom_forward, 0)

    for g in range(groups):
        tall[g, :nv] = unit
        tall[g, nv:] = jnp.zeros((nv, nv), F32)
        wide_state[g] = second_unit

    def hom_backward(i, carry):
        x = cells - 1 - i
        for g in range(groups):
            m = hom[g, x + 1] + mul(get(bt, g, x), split(wide_state[g]))
            resp[g, 0, x], resp[g, 1, x] = split(m)
            wide_state[g] = m
            now = split(
                jnp.concatenate([tall[g, :nv], omega[g, x] + tall[g, nv:]], axis=0)
            )
            put(gain, g, x, split(mul(now, get(vt, g, x))))
            tall[g] = mul(now, get(ft, g, x))
        return carry

    loop(cells, hom_backward, 0)
    for g in range(groups):
        gmap[gx, g * nv : (g + 1) * nv] = wide_state[g]
    gmap[gx, groups * nv :] = jnp.concatenate(
        [hom[g, cells][:, :nv] for g in range(groups)], axis=1
    )

    def share(buffer, send, recv, slot, target, k):
        return pltpu.make_async_remote_copy(
            src_ref=buffer.at[slot],
            dst_ref=buffer.at[slot],
            send_sem=send.at[k],
            recv_sem=recv.at[slot],
            device_id=(target, yz),
            device_id_type=MESH,
        )

    def offer(*where):
        for k in range(1, half):
            share(*where, gx, peer(k), k).start()
        share(*where, gx, partner, 0).start()

    def relay(*where):
        for k in range(1, half):
            share(*where, peer(k), peer(k), k).wait_recv()
            share(*where, peer(k), partner, half + k).start()

    def collect(*where):
        share(*where, partner, partner, 0).wait_recv()
        for k in range(1, half):
            share(*where, lax.rem(partner + 2 * k, n_gx), partner, half + k).wait_recv()

    def release(*where):
        share(*where, gx, partner, 0).wait_send()
        for k in range(1, half):
            share(*where, gx, peer(k), k).wait_send()
            share(*where, peer(k), partner, half + k).wait_send()

    maps = (gmap, map_send, map_recv)
    offer(*maps)

    edge = cells - chunk

    def weight(g, x):
        kind = cat[x][g : g + 1]
        return jnp.where(kind == 0, 1.0, jnp.where(kind == 2, 0.5, 0.0))

    def slope(g, x):
        if g == 0:
            return 8.0 * res[x, 1] + low[g, x] - high[g, x]
        return low[g, x] + high[g, x] - 8.0 * res[x, 0]

    def arrive(g, c):
        @pl.when(has_low)
        def _():
            halo(0, g, c).wait_recv()

        @pl.when(has_high)
        def _():
            halo(1, g, c).wait_recv()

    def local_forward(g, c, state, gather):
        for x in range(c * chunk, (c + 1) * chunk):
            force = split(weight(g, x) * (res[x, g] + mul(held(g, 0), split(slope(g, x)))))
            driven = mul(get(vt, g, x), force)
            state = driven + mul(get(ft, g, x), split(state))
            cs[g, x] = state
            if gather:
                acc[g] += mul(get(gain, g, x), force)
        return state

    def parcel(g, target):
        return pltpu.make_async_remote_copy(
            src_ref=given.at[g, target],
            dst_ref=taken.at[g, gx],
            send_sem=vec_send.at[g, target],
            recv_sem=vec_recv.at[g, gx],
            device_id=(target, yz),
            device_id_type=MESH,
        )

    def receive(g, source):
        pltpu.make_async_remote_copy(
            src_ref=given.at[g, source],
            dst_ref=taken.at[g, source],
            send_sem=vec_send.at[g, source],
            recv_sem=vec_recv.at[g, source],
            device_id=(source, yz),
            device_id_type=MESH,
        ).wait_recv()

    def dispatch(g):
        ah, al = split(acc[g])
        for t in range(n_gx // 4):
            zh = send_map[g, 0, 4 * t : 4 * t + 4].reshape(4 * nv, 2 * nv)
            zl = send_map[g, 1, 4 * t : 4 * t + 4].reshape(4 * nv, 2 * nv)
            given[g, 4 * t : 4 * t + 4] = mul((zh, zl), (ah, al)).reshape(4, nv, nz)
        for k in range(1, n_gx):
            parcel(g, lax.rem(gx + k, n_gx)).start()

    def local_backward(g):
        into_state[g] = cs[g, cells - 1]

        def backward(i, carry):
            x = cells - 2 - i
            state = cs[g, x] + mul(get(bt, g, x), split(into_state[g]))
            into_state[g] = state
            cs[g, x] = state
            return carry

        lax.fori_loop(0, cells - 1, backward, 0)

    def finish(g):
        head = jnp.zeros((nv, nz), F32)
        tail = given[g, gx]
        for k in range(1, n_gx):
            j = lax.rem(gx + k, n_gx)
            receive(g, j)
            value = taken[g, j]
            head = head + jnp.where(j < gx, value, 0.0)
            tail = tail + jnp.where(j < gx, 0.0, value)
        both = split(jnp.concatenate([head, tail], axis=0))
        block = next(c for c in (4, 3, 2, 1) if cells % c == 0)
        for x in range(0, cells, block):
            maps_here = tuple(
                resp[g, n, x : x + block].reshape(block * nv, 2 * nv) for n in range(2)
            )
            fix = mul(maps_here, both).reshape(block, nv, nz)
            for k in range(block):
                value = cs[g, x + k] + fix[k]
                out[x + k, g] = jnp.where(cat[x + k][g : g + 1] != 1, value, 0.0)

    for g in range(groups):
        acc[g] = jnp.zeros((2 * nv, nz), F32)

    state = jnp.zeros((nv, nz), F32)
    for c in range(pieces):
        arrive(0, c)
        state = local_forward(0, c, state, True)

    relay(*maps)
    collect(*maps)

    for g in range(groups):
        mirror[g] = jnp.zeros((nv, nv), F32)
        ahead[g, 0] = unit
        behind[g, n_gx] = unit

    def chains(t, carry):
        i = n_gx - 1 - t
        p_up = gmap[t, groups * nv :]
        p_down = gmap[i, groups * nv :]
        grow = t > gx
        shrink = i < gx
        here = i == gx
        for g in range(groups):
            cols = slice(g * nv, (g + 1) * nv)
            step = mul(split(p_up[:, cols]), split(ahead[g, t]))
            ahead[g, t + 1] = jnp.where(grow, step, unit)
            rq = gmap[i, g * nv : (g + 1) * nv]
            q = split(rq[:, nv:])
            step = mul(q, split(behind[g, i + 1]))
            behind[g, i] = jnp.where(shrink, step, unit)
            s_now = mirror[g]
            qs = mul(q, split(s_now))
            hom[g, i] = jnp.concatenate([qs, s_now], axis=1)
            mirror[g] = rq[:, :nv] + mul(split(qs), split(p_down[:, cols]))
        return carry

    loop(n_gx, chains, 0)

    for g in range(groups):
        pair = hom[g, gx]
        qs = pair[:, :nv]
        s_now = pair[:, nv:]
        zero = jnp.zeros((nv, nv), F32)
        p_here = gmap[gx, groups * nv :][:, g * nv : (g + 1) * nv]
        sp = mul(split(s_now), split(p_here))
        left = jnp.concatenate([qs, unit], axis=1)
        for i in range(n_gx):
            m = mul(split(behind[g, i + 1]), split(left))
            m = jnp.where(i < gx, m, jnp.concatenate([ahead[g, i], zero], axis=1))
            m = jnp.where(gx == i, jnp.concatenate([s_now, zero], axis=1), m)
            send_map[g, 0, i], send_map[g, 1, i] = split(m)
        turn = split(
            jnp.concatenate(
                [first_unit, jnp.concatenate([sp, unit], axis=1)], axis=0
            )
        )
        block = next(c for c in (4, 3, 2, 1) if cells % c == 0)
        for x in range(0, cells, block):
            maps_here = tuple(
                resp[g, n, x : x + block].reshape(block * nv, 2 * nv) for n in range(2)
            )
            fixed = split(mul(maps_here, turn))
            for n in range(2):
                resp[g, n, x : x + block] = fixed[n].reshape(block, nv, 2 * nv)

    dispatch(0)
    local_backward(0)

    last = groups - 1
    for n in range(chunk):
        x = edge + n
        fast[n, 0], fast[n, 1] = split(mul(get(gain, last, x), held(last, 0)))
        acc[last] += mul(get(gain, last, x), split(weight(last, x) * res[x, last]))

    state = jnp.zeros((nv, nz), F32)
    for c in range(pieces - 1):
        arrive(last, c)
        state = local_forward(last, c, state, True)
    arrive(last, pieces - 1)
    for n in range(chunk):
        x = edge + n
        acc[last] += mul((fast[n, 0], fast[n, 1]), split(weight(last, x) * slope(last, x)))
    dispatch(last)
    local_forward(last, pieces - 1, state, False)
    local_backward(last)
    for g in range(groups):
        finish(g)

    @pl.when(has_high)
    def _():
        for g in range(groups):
            for c in range(pieces):
                halo(0, g, c).wait_send()

    @pl.when(has_low)
    def _():
        for g in range(groups):
            for c in range(pieces):
                halo(1, g, c).wait_send()

    release(*maps)
    for g in range(groups):
        for k in range(1, n_gx):
            parcel(g, lax.rem(gx + k, n_gx)).wait_send()


def per_device(n_gx, n_yz, residual, inverses, upwind, downwind, flux_y, kinds, volume_category):
    cells, groups, nv, nz = residual.shape
    chunk = next(c for c in (3, 4, 2, 1) if cells % c == 0)
    pieces = cells // chunk
    hbm = pl.BlockSpec(memory_space=pltpu.HBM)
    operands = (residual, inverses, upwind, downwind, flux_y, volume_category, kinds)
    square = pltpu.VMEM((groups, cells, 2, nv, nv), BF16)
    wide = pltpu.VMEM((groups, cells, nv, nz), F32)
    return pl.pallas_call(
        functools.partial(kernel, n_gx, n_yz, chunk),
        out_shape=jax.ShapeDtypeStruct(residual.shape, F32),
        in_specs=[hbm] * 7,
        out_specs=pl.BlockSpec(memory_space=pltpu.VMEM),
        scratch_shapes=[pltpu.VMEM(a.shape, a.dtype) for a in operands[:-1]]
        + [
            pltpu.SMEM(kinds.shape, kinds.dtype),
            pltpu.VMEM((2, cells, nv, nz), F32),
            wide,
            wide,
            pltpu.VMEM((groups, 3, 2, nv, nv), BF16),
            square,
            square,
            square,
            pltpu.VMEM((groups, max(cells, n_gx) + 1, nv, 2 * nv), F32),
            pltpu.VMEM((groups, cells + 1, nv, nv), F32),
            pltpu.VMEM((groups, cells, 2, 2 * nv, nv), BF16),
            pltpu.VMEM((chunk, 2, 2 * nv, nv), BF16),
            pltpu.VMEM((groups, 2, cells, nv, 2 * nv), BF16),
            wide,
            pltpu.VMEM((groups, 2 * nv, nz), F32),
            pltpu.VMEM((n_gx, (groups + 1) * nv, 2 * nv), F32),
            pltpu.VMEM((groups, n_gx, nv, nz), F32),
            pltpu.VMEM((groups, n_gx, nv, nz), F32),
            pltpu.VMEM((groups, 2, n_gx, nv, 2 * nv), BF16),
            pltpu.VMEM((groups, n_gx + 1, nv, nv), F32),
            pltpu.VMEM((groups, n_gx + 1, nv, nv), F32),
            pltpu.VMEM((groups, nv, nv), F32),
            pltpu.VMEM((groups, nv, 2 * nv), F32),
            pltpu.VMEM((groups, 2 * nv, nv), F32),
            pltpu.VMEM((groups, nv, nz), F32),
            pltpu.SemaphoreType.DMA((7,)),
            pltpu.SemaphoreType.DMA((2, groups, pieces)),
            pltpu.SemaphoreType.DMA((2, groups, pieces)),
            pltpu.SemaphoreType.DMA((n_gx,)),
            pltpu.SemaphoreType.DMA((n_gx,)),
            pltpu.SemaphoreType.DMA((groups, n_gx)),
            pltpu.SemaphoreType.DMA((groups, n_gx)),
        ],
        compiler_params=pltpu.CompilerParams(
            collective_id=0, has_side_effects=True, vmem_limit_bytes=48 * 1024 * 1024
        ),
    )(*(pltpu.with_memory_space_constraint(a, pltpu.HBM) for a in operands))


def solution(mesh):
    in_specs = (
        P("gx", "yz", None, None),
        P("gx", "yz", None, None),
        P(),
        P(),
        P(),
        P("yz"),
        P("gx", "yz", None),
    )
    out_specs = P("gx", "yz", None, None)
    return jax.shard_map(
        functools.partial(per_device, mesh.shape["gx"], mesh.shape["yz"]),
        mesh=mesh,
        in_specs=in_specs,
        out_specs=out_specs,
        check_vma=False,
    )
```

```python
import functools

import jax
import jax.numpy as jnp
from jax import lax
from jax.experimental import pallas as pl
from jax.experimental.pallas import tpu as pltpu
from jax.sharding import PartitionSpec as P

MESH = pl.DeviceIdType.MESH
F32 = jnp.float32
BF16 = jnp.bfloat16


def split(a):
    high = a.astype(BF16)
    return high, (a - high.astype(F32)).astype(BF16)


def mul(a, b):
    ah, al = a
    bh, bl = b
    d = functools.partial(jnp.dot, preferred_element_type=F32)
    return d(ah, bh) + (d(ah, bl) + d(al, bh))


def loop(count, body, carry, unroll=1):
    unroll = unroll if count % unroll == 0 else 1

    def several(i, carry):
        for u in range(unroll):
            carry = body(i * unroll + u, carry)
        return carry

    return lax.fori_loop(0, count // unroll, several, carry)


def kernel(
    n_gx, n_yz, chunk, res_hbm, inv_hbm, up_hbm, down_hbm, flux_hbm, cat_hbm, kinds_hbm, out,
    res, inv, up, down, flux, cat, kinds,
    snd, low, high, table, vt, ft, bt, hom, omega, path, echo, gain, fast, resp, cs, acc, gmap, given, taken,
    send_map, ahead, behind, mirror, wide_state, tall, into_state,
    load_sem, halo_send, halo_recv, map_send, map_recv, vec_send, vec_recv,
):
    cells, groups, nv, nz = res.shape
    half = n_gx // 2
    pieces = cells // chunk
    gx = lax.axis_index("gx")
    yz = lax.axis_index("yz")
    partner = gx + 1 - 2 * lax.rem(gx, 2)
    has_low = yz > 0
    has_high = yz < n_yz - 1

    loads = [
        pltpu.make_async_copy(source, target, load_sem.at[n])
        for n, (source, target) in enumerate(
            (
                (res_hbm, res), (inv_hbm, inv), (up_hbm, up), (down_hbm, down),
                (flux_hbm, flux), (cat_hbm, cat), (kinds_hbm, kinds),
            )
        )
    ]
    for load in loads:
        load.start()

    def peer(k):
        return lax.rem(gx + 2 * k, n_gx)

    barrier = pltpu.get_barrier_semaphore()
    for k in range(1, n_gx):
        pl.semaphore_signal(
            barrier, inc=1, device_id=(lax.rem(gx + k, n_gx), yz), device_id_type=MESH
        )

    @pl.when(has_low)
    def _():
        pl.semaphore_signal(barrier, inc=1, device_id=(gx, yz - 1), device_id_type=MESH)

    @pl.when(has_high)
    def _():
        pl.semaphore_signal(barrier, inc=1, device_id=(gx, yz + 1), device_id_type=MESH)

    pl.semaphore_wait(barrier, n_gx - 1 + jnp.where(has_low, 1, 0) + jnp.where(has_high, 1, 0))

    def halo(direction, g, c):
        part = pl.ds(c * chunk, chunk)
        if direction == 0:
            src = snd.at[0, part] if g == 0 else res_hbm.at[part, 1]
            dst, where = low, yz + 1
        else:
            src = res_hbm.at[part, 0] if g == 0 else snd.at[1, part]
            dst, where = high, yz - 1
        return pltpu.make_async_remote_copy(
            src_ref=src,
            dst_ref=dst.at[g, part],
            send_sem=halo_send.at[direction, g, c],
            recv_sem=halo_recv.at[direction, g, c],
            device_id=(gx, where),
            device_id_type=MESH,
        )

    @pl.when(has_low)
    def _():
        for c in range(pieces):
            halo(1, 0, c).start()

    loads[0].wait()

    for c in range(pieces):
        for x in range(c * chunk, (c + 1) * chunk):
            snd[0, x] = res[x, 0] - 8.0 * res[x, 1]

        @pl.when(has_high)
        def _():
            halo(0, 0, c).start()

    @pl.when(has_high)
    def _():
        for c in range(pieces):
            halo(0, 1, c).start()

    for c in range(pieces):
        for x in range(c * chunk, (c + 1) * chunk):
            snd[1, x] = 8.0 * res[x, 0] - res[x, 1]

        @pl.when(has_low)
        def _():
            halo(1, 1, c).start()

    @pl.when(jnp.logical_not(has_low))
    def _():
        low[...] = jnp.zeros_like(low)

    @pl.when(jnp.logical_not(has_high))
    def _():
        high[...] = jnp.zeros_like(high)

    for load in loads[1:]:
        load.wait()

    for g in range(groups):
        kind = kinds[g]
        for n, block in enumerate((flux[kind] * (1.0 / 12.0), -up[kind], -down[kind])):
            table[g, n, 0], table[g, n, 1] = split(block.T)

    def held(g, n):
        return table[g, n, 0], table[g, n, 1]

    def put(ref, g, x, pair):
        ref[g, x, 0], ref[g, x, 1] = pair

    def get(ref, g, x):
        return ref[g, x, 0], ref[g, x, 1]

    def steps(x, carry):
        for g in range(groups):
            v = split(inv[x, g].T)
            put(vt, g, x, v)
            put(ft, g, x, split(mul(v, held(g, 1))))
            put(bt, g, x, split(mul(v, held(g, 2))))
        return carry

    loop(cells, steps, 0, 4)

    row = lax.broadcasted_iota(jnp.int32, (nv, 2 * nv), 0)
    col = lax.broadcasted_iota(jnp.int32, (nv, 2 * nv), 1)
    first_unit = (row == col).astype(F32)
    second_unit = (row + nv == col).astype(F32)
    square_row = lax.broadcasted_iota(jnp.int32, (nv, nv), 0)
    square_col = lax.broadcasted_iota(jnp.int32, (nv, nv), 1)
    unit = (square_row == square_col).astype(F32)
    for g in range(groups):
        hom[g, 0] = first_unit
        omega[g, 0] = unit
        path[g] = jnp.zeros((2, nv, nv), BF16)
        echo[g] = jnp.zeros((nv, 2 * nv), F32)

    def hom_forward(x, carry):
        for g in range(groups):
            onward = split(omega[g, x])
            ahead_of = tuple(
                jnp.concatenate([ft[g, x, n], path[g, n]], axis=0) for n in range(2)
            )
            both = mul(ahead_of, split(hom[g, x]))
            hom[g, x + 1] = both[:nv]
            echo[g] += both[nv:]
            omega[g, x + 1] = mul(onward, get(bt, g, x))
            path[g, 0], path[g, 1] = onward
        return carry

    loop(cells, hom_forward, 0)
    for g in range(groups):
        total = echo[g] + mul((path[g, 0], path[g, 1]), split(hom[g, cells]))
        gmap[gx, g * nv : (g + 1) * nv] = jnp.concatenate(
            [total[:, :nv], omega[g, cells]], axis=1
        )
    gmap[gx, groups * nv :] = jnp.concatenate(
        [hom[g, cells][:, :nv] for g in range(groups)], axis=1
    )

    def share(buffer, send, recv, slot, target, k):
        return pltpu.make_async_remote_copy(
            src_ref=buffer.at[slot],
            dst_ref=buffer.at[slot],
            send_sem=send.at[k],
            recv_sem=recv.at[slot],
            device_id=(target, yz),
            device_id_type=MESH,
        )

    def offer(*where):
        for k in range(1, half):
            share(*where, gx, peer(k), k).start()
        share(*where, gx, partner, 0).start()

    def relay(*where):
        for k in range(1, half):
            share(*where, peer(k), peer(k), k).wait_recv()
            share(*where, peer(k), partner, half + k).start()

    def collect(*where):
        share(*where, partner, partner, 0).wait_recv()
        for k in range(1, half):
            share(*where, lax.rem(partner + 2 * k, n_gx), partner, half + k).wait_recv()

    def release(*where):
        share(*where, gx, partner, 0).wait_send()
        for k in range(1, half):
            share(*where, gx, peer(k), k).wait_send()
            share(*where, peer(k), partner, half + k).wait_send()

    maps = (gmap, map_send, map_recv)
    offer(*maps)

    for g in range(groups):
        tall[g, :nv] = unit
        tall[g, nv:] = jnp.zeros((nv, nv), F32)
        wide_state[g] = second_unit

    def hom_backward(i, carry):
        x = cells - 1 - i
        for g in range(groups):
            m = hom[g, x + 1] + mul(get(bt, g, x), split(wide_state[g]))
            resp[g, 0, x], resp[g, 1, x] = split(m)
            wide_state[g] = m
            now = split(
                jnp.concatenate([tall[g, :nv], omega[g, x] + tall[g, nv:]], axis=0)
            )
            put(gain, g, x, split(mul(now, get(vt, g, x))))
            tall[g] = mul(now, get(ft, g, x))
        return carry

    loop(cells, hom_backward, 0)

    edge = cells - chunk

    def weight(g, x):
        kind = cat[x][g : g + 1]
        return jnp.where(kind == 0, 1.0, jnp.where(kind == 2, 0.5, 0.0))

    def slope(g, x):
        if g == 0:
            return 8.0 * res[x, 1] + low[g, x] - high[g, x]
        return low[g, x] + high[g, x] - 8.0 * res[x, 0]

    def arrive(g, c):
        @pl.when(has_low)
        def _():
            halo(0, g, c).wait_recv()

        @pl.when(has_high)
        def _():
            halo(1, g, c).wait_recv()

    def local_forward(g, c, gather):
        for x in range(c * chunk, (c + 1) * chunk):
            force = split(weight(g, x) * (res[x, g] + mul(held(g, 0), split(slope(g, x)))))
            cs[g, x] = mul(get(vt, g, x), force)
            if gather:
                acc[g] += mul(get(gain, g, x), force)

    def parcel(g, target):
        return pltpu.make_async_remote_copy(
            src_ref=given.at[g, target],
            dst_ref=taken.at[g, gx],
            send_sem=vec_send.at[g, target],
            recv_sem=vec_recv.at[g, gx],
            device_id=(target, yz),
            device_id_type=MESH,
        )

    def receive(g, source):
        pltpu.make_async_remote_copy(
            src_ref=given.at[g, source],
            dst_ref=taken.at[g, source],
            send_sem=vec_send.at[g, source],
            recv_sem=vec_recv.at[g, source],
            device_id=(source, yz),
            device_id_type=MESH,
        ).wait_recv()

    def dispatch(g):
        ah, al = split(acc[g])
        for t in range(n_gx // 4):
            zh = send_map[g, 0, 4 * t : 4 * t + 4].reshape(4 * nv, 2 * nv)
            zl = send_map[g, 1, 4 * t : 4 * t + 4].reshape(4 * nv, 2 * nv)
            given[g, 4 * t : 4 * t + 4] = mul((zh, zl), (ah, al)).reshape(4, nv, nz)
        for k in range(1, n_gx):
            parcel(g, lax.rem(gx + k, n_gx)).start()

    def sweep():
        for g in range(groups):
            into_state[g] = cs[g, 0]

        def forward(i, carry):
            for g in range(groups):
                state = cs[g, i + 1] + mul(get(ft, g, i + 1), split(into_state[g]))
                into_state[g] = state
                cs[g, i + 1] = state
            return carry

        lax.fori_loop(0, cells - 1, forward, 0)

        def backward(i, carry):
            x = cells - 2 - i
            for g in range(groups):
                state = cs[g, x] + mul(get(bt, g, x), split(into_state[g]))
                into_state[g] = state
                cs[g, x] = state
            return carry

        lax.fori_loop(0, cells - 1, backward, 0)

    def finish(g):
        head = jnp.zeros((nv, nz), F32)
        tail = given[g, gx]
        for k in range(1, n_gx):
            j = lax.rem(gx + k, n_gx)
            receive(g, j)
            value = taken[g, j]
            head = head + jnp.where(j < gx, value, 0.0)
            tail = tail + jnp.where(j < gx, 0.0, value)
        both = split(jnp.concatenate([head, tail], axis=0))
        block = next(c for c in (4, 3, 2, 1) if cells % c == 0)
        for x in range(0, cells, block):
            maps_here = tuple(
                resp[g, n, x : x + block].reshape(block * nv, 2 * nv) for n in range(2)
            )
            fix = mul(maps_here, both).reshape(block, nv, nz)
            for k in range(block):
                value = cs[g, x + k] + fix[k]
                out[x + k, g] = jnp.where(cat[x + k][g : g + 1] != 1, value, 0.0)

    for g in range(groups):
        acc[g] = jnp.zeros((2 * nv, nz), F32)

    for c in range(pieces):
        arrive(0, c)
        local_forward(0, c, True)

    relay(*maps)
    collect(*maps)

    for g in range(groups):
        mirror[g] = jnp.zeros((nv, nv), F32)
        ahead[g, 0] = unit
        behind[g, n_gx] = unit

    def chains(t, carry):
        i = n_gx - 1 - t
        p_up = gmap[t, groups * nv :]
        p_down = gmap[i, groups * nv :]
        grow = t > gx
        shrink = i < gx
        here = i == gx
        for g in range(groups):
            cols = slice(g * nv, (g + 1) * nv)
            step = mul(split(p_up[:, cols]), split(ahead[g, t]))
            ahead[g, t + 1] = jnp.where(grow, step, unit)
            rq = gmap[i, g * nv : (g + 1) * nv]
            q = split(rq[:, nv:])
            step = mul(q, split(behind[g, i + 1]))
            behind[g, i] = jnp.where(shrink, step, unit)
            s_now = mirror[g]
            qs = mul(q, split(s_now))
            hom[g, i] = jnp.concatenate([qs, s_now], axis=1)
            mirror[g] = rq[:, :nv] + mul(split(qs), split(p_down[:, cols]))
        return carry

    loop(n_gx, chains, 0)

    for g in range(groups):
        pair = hom[g, gx]
        qs = pair[:, :nv]
        s_now = pair[:, nv:]
        zero = jnp.zeros((nv, nv), F32)
        p_here = gmap[gx, groups * nv :][:, g * nv : (g + 1) * nv]
        sp = mul(split(s_now), split(p_here))
        left = jnp.concatenate([qs, unit], axis=1)
        for i in range(n_gx):
            m = mul(split(behind[g, i + 1]), split(left))
            m = jnp.where(i < gx, m, jnp.concatenate([ahead[g, i], zero], axis=1))
            m = jnp.where(gx == i, jnp.concatenate([s_now, zero], axis=1), m)
            send_map[g, 0, i], send_map[g, 1, i] = split(m)
        turn = split(
            jnp.concatenate(
                [first_unit, jnp.concatenate([sp, unit], axis=1)], axis=0
            )
        )
        block = next(c for c in (4, 3, 2, 1) if cells % c == 0)
        for x in range(0, cells, block):
            maps_here = tuple(
                resp[g, n, x : x + block].reshape(block * nv, 2 * nv) for n in range(2)
            )
            fixed = split(mul(maps_here, turn))
            for n in range(2):
                resp[g, n, x : x + block] = fixed[n].reshape(block, nv, 2 * nv)

    dispatch(0)

    last = groups - 1
    for n in range(chunk):
        x = edge + n
        fast[n, 0], fast[n, 1] = split(mul(get(gain, last, x), held(last, 0)))
        acc[last] += mul(get(gain, last, x), split(weight(last, x) * res[x, last]))

    for c in range(pieces - 1):
        arrive(last, c)
        local_forward(last, c, True)
    arrive(last, pieces - 1)
    for n in range(chunk):
        x = edge + n
        acc[last] += mul((fast[n, 0], fast[n, 1]), split(weight(last, x) * slope(last, x)))
    dispatch(last)
    local_forward(last, pieces - 1, False)
    sweep()
    for g in range(groups):
        finish(g)

    @pl.when(has_high)
    def _():
        for g in range(groups):
            for c in range(pieces):
                halo(0, g, c).wait_send()

    @pl.when(has_low)
    def _():
        for g in range(groups):
            for c in range(pieces):
                halo(1, g, c).wait_send()

    release(*maps)
    for g in range(groups):
        for k in range(1, n_gx):
            parcel(g, lax.rem(gx + k, n_gx)).wait_send()


def per_device(n_gx, n_yz, residual, inverses, upwind, downwind, flux_y, kinds, volume_category):
    cells, groups, nv, nz = residual.shape
    chunk = next(c for c in (3, 4, 2, 1) if cells % c == 0)
    pieces = cells // chunk
    hbm = pl.BlockSpec(memory_space=pltpu.HBM)
    operands = (residual, inverses, upwind, downwind, flux_y, volume_category, kinds)
    square = pltpu.VMEM((groups, cells, 2, nv, nv), BF16)
    wide = pltpu.VMEM((groups, cells, nv, nz), F32)
    return pl.pallas_call(
        functools.partial(kernel, n_gx, n_yz, chunk),
        out_shape=jax.ShapeDtypeStruct(residual.shape, F32),
        in_specs=[hbm] * 7,
        out_specs=pl.BlockSpec(memory_space=pltpu.VMEM),
        scratch_shapes=[pltpu.VMEM(a.shape, a.dtype) for a in operands[:-1]]
        + [
            pltpu.SMEM(kinds.shape, kinds.dtype),
            pltpu.VMEM((2, cells, nv, nz), F32),
            wide,
            wide,
            pltpu.VMEM((groups, 3, 2, nv, nv), BF16),
            square,
            square,
            square,
            pltpu.VMEM((groups, max(cells, n_gx) + 1, nv, 2 * nv), F32),
            pltpu.VMEM((groups, cells + 1, nv, nv), F32),
            pltpu.VMEM((groups, 2, nv, nv), BF16),
            pltpu.VMEM((groups, nv, 2 * nv), F32),
            pltpu.VMEM((groups, cells, 2, 2 * nv, nv), BF16),
            pltpu.VMEM((chunk, 2, 2 * nv, nv), BF16),
            pltpu.VMEM((groups, 2, cells, nv, 2 * nv), BF16),
            wide,
            pltpu.VMEM((groups, 2 * nv, nz), F32),
            pltpu.VMEM((n_gx, (groups + 1) * nv, 2 * nv), F32),
            pltpu.VMEM((groups, n_gx, nv, nz), F32),
            pltpu.VMEM((groups, n_gx, nv, nz), F32),
            pltpu.VMEM((groups, 2, n_gx, nv, 2 * nv), BF16),
            pltpu.VMEM((groups, n_gx + 1, nv, nv), F32),
            pltpu.VMEM((groups, n_gx + 1, nv, nv), F32),
            pltpu.VMEM((groups, nv, nv), F32),
            pltpu.VMEM((groups, nv, 2 * nv), F32),
            pltpu.VMEM((groups, 2 * nv, nv), F32),
            pltpu.VMEM((groups, nv, nz), F32),
            pltpu.SemaphoreType.DMA((7,)),
            pltpu.SemaphoreType.DMA((2, groups, pieces)),
            pltpu.SemaphoreType.DMA((2, groups, pieces)),
            pltpu.SemaphoreType.DMA((n_gx,)),
            pltpu.SemaphoreType.DMA((n_gx,)),
            pltpu.SemaphoreType.DMA((groups, n_gx)),
            pltpu.SemaphoreType.DMA((groups, n_gx)),
        ],
        compiler_params=pltpu.CompilerParams(
            collective_id=0, has_side_effects=True, vmem_limit_bytes=48 * 1024 * 1024
        ),
    )(*(pltpu.with_memory_space_constraint(a, pltpu.HBM) for a in operands))


def solution(mesh):
    in_specs = (
        P("gx", "yz", None, None),
        P("gx", "yz", None, None),
        P(),
        P(),
        P(),
        P("yz"),
        P("gx", "yz", None),
    )
    out_specs = P("gx", "yz", None, None)
    return jax.shard_map(
        functools.partial(per_device, mesh.shape["gx"], mesh.shape["yz"]),
        mesh=mesh,
        in_specs=in_specs,
        out_specs=out_specs,
        check_vma=False,
    )
```

```python
import functools

import jax
import jax.numpy as jnp
from jax import lax
from jax.experimental import pallas as pl
from jax.experimental.pallas import tpu as pltpu
from jax.sharding import PartitionSpec as P

MESH = pl.DeviceIdType.MESH
F32 = jnp.float32
BF16 = jnp.bfloat16


def split(a):
    high = a.astype(BF16)
    return high, (a - high.astype(F32)).astype(BF16)


def mul(a, b):
    ah, al = a
    bh, bl = b
    d = functools.partial(jnp.dot, preferred_element_type=F32)
    return d(ah, bh) + (d(ah, bl) + d(al, bh))


def loop(count, body, carry, unroll=1):
    unroll = unroll if count % unroll == 0 else 1

    def several(i, carry):
        for u in range(unroll):
            carry = body(i * unroll + u, carry)
        return carry

    return lax.fori_loop(0, count // unroll, several, carry)


def kernel(
    n_gx, n_yz, chunk, res_hbm, inv_hbm, up_hbm, down_hbm, flux_hbm, cat_hbm, kinds_hbm, out,
    res, inv, up, down, flux, cat, kinds,
    snd, low, high, table, vt, ft, bt, hom, omega, path, echo, gain, fast, resp, cs, acc, gmap, given, taken,
    send_map, ahead, behind, mirror, wide_state, tall, into_state,
    load_sem, halo_send, halo_recv, map_send, map_recv, vec_send, vec_recv,
):
    cells, groups, nv, nz = res.shape
    half = n_gx // 2
    pieces = cells // chunk
    gx = lax.axis_index("gx")
    yz = lax.axis_index("yz")
    partner = gx + 1 - 2 * lax.rem(gx, 2)
    has_low = yz > 0
    has_high = yz < n_yz - 1

    loads = [
        pltpu.make_async_copy(source, target, load_sem.at[n])
        for n, (source, target) in enumerate(
            (
                (res_hbm, res), (inv_hbm, inv), (up_hbm, up), (down_hbm, down),
                (flux_hbm, flux), (cat_hbm, cat), (kinds_hbm, kinds),
            )
        )
    ]
    for load in loads:
        load.start()

    def peer(k):
        return lax.rem(gx + 2 * k, n_gx)

    barrier = pltpu.get_barrier_semaphore()
    for k in range(1, n_gx):
        pl.semaphore_signal(
            barrier, inc=1, device_id=(lax.rem(gx + k, n_gx), yz), device_id_type=MESH
        )

    @pl.when(has_low)
    def _():
        pl.semaphore_signal(barrier, inc=1, device_id=(gx, yz - 1), device_id_type=MESH)

    @pl.when(has_high)
    def _():
        pl.semaphore_signal(barrier, inc=1, device_id=(gx, yz + 1), device_id_type=MESH)

    pl.semaphore_wait(barrier, n_gx - 1 + jnp.where(has_low, 1, 0) + jnp.where(has_high, 1, 0))

    def halo(direction, g, c):
        part = pl.ds(c * chunk, chunk)
        if direction == 0:
            src = snd.at[0, part] if g == 0 else res_hbm.at[part, 1]
            dst, where = low, yz + 1
        else:
            src = res_hbm.at[part, 0] if g == 0 else snd.at[1, part]
            dst, where = high, yz - 1
        return pltpu.make_async_remote_copy(
            src_ref=src,
            dst_ref=dst.at[g, part],
            send_sem=halo_send.at[direction, g, c],
            recv_sem=halo_recv.at[direction, g, c],
            device_id=(gx, where),
            device_id_type=MESH,
        )

    @pl.when(has_low)
    def _():
        for c in range(pieces):
            halo(1, 0, c).start()

    loads[0].wait()

    for c in range(pieces):
        for x in range(c * chunk, (c + 1) * chunk):
            snd[0, x] = res[x, 0] - 8.0 * res[x, 1]

        @pl.when(has_high)
        def _():
            halo(0, 0, c).start()

    @pl.when(has_high)
    def _():
        for c in range(pieces):
            halo(0, 1, c).start()

    for c in range(pieces):
        for x in range(c * chunk, (c + 1) * chunk):
            snd[1, x] = 8.0 * res[x, 0] - res[x, 1]

        @pl.when(has_low)
        def _():
            halo(1, 1, c).start()

    @pl.when(jnp.logical_not(has_low))
    def _():
        low[...] = jnp.zeros_like(low)

    @pl.when(jnp.logical_not(has_high))
    def _():
        high[...] = jnp.zeros_like(high)

    for load in loads[1:]:
        load.wait()

    for g in range(groups):
        kind = kinds[g]
        for n, block in enumerate((flux[kind] * (1.0 / 12.0), -up[kind], -down[kind])):
            table[g, n, 0], table[g, n, 1] = split(block.T)

    def held(g, n):
        return table[g, n, 0], table[g, n, 1]

    def put(ref, g, x, pair):
        ref[g, x, 0], ref[g, x, 1] = pair

    def get(ref, g, x):
        return ref[g, x, 0], ref[g, x, 1]

    def steps(x, carry):
        for g in range(groups):
            v = split(inv[x, g].T)
            put(vt, g, x, v)
            put(ft, g, x, split(mul(v, held(g, 1))))
            put(bt, g, x, split(mul(v, held(g, 2))))
        return carry

    loop(cells, steps, 0, 4)

    row = lax.broadcasted_iota(jnp.int32, (nv, 2 * nv), 0)
    col = lax.broadcasted_iota(jnp.int32, (nv, 2 * nv), 1)
    first_unit = (row == col).astype(F32)
    second_unit = (row + nv == col).astype(F32)
    square_row = lax.broadcasted_iota(jnp.int32, (nv, nv), 0)
    square_col = lax.broadcasted_iota(jnp.int32, (nv, nv), 1)
    unit = (square_row == square_col).astype(F32)
    for g in range(groups):
        hom[g, 0] = first_unit
        omega[g, 0] = unit
        path[g] = jnp.zeros((2, nv, nv), BF16)
        echo[g] = jnp.zeros((nv, 2 * nv), F32)

    def hom_forward(x, carry):
        for g in range(groups):
            onward = split(omega[g, x])
            ahead_of = tuple(
                jnp.concatenate([ft[g, x, n], path[g, n]], axis=0) for n in range(2)
            )
            both = mul(ahead_of, split(hom[g, x]))
            hom[g, x + 1] = both[:nv]
            echo[g] += both[nv:]
            omega[g, x + 1] = mul(onward, get(bt, g, x))
            path[g, 0], path[g, 1] = onward
        return carry

    loop(cells, hom_forward, 0)
    for g in range(groups):
        total = echo[g] + mul((path[g, 0], path[g, 1]), split(hom[g, cells]))
        gmap[gx, g * nv : (g + 1) * nv] = jnp.concatenate(
            [total[:, :nv], omega[g, cells]], axis=1
        )
    gmap[gx, groups * nv :] = jnp.concatenate(
        [hom[g, cells][:, :nv] for g in range(groups)], axis=1
    )

    def share(buffer, send, recv, slot, target, k):
        return pltpu.make_async_remote_copy(
            src_ref=buffer.at[slot],
            dst_ref=buffer.at[slot],
            send_sem=send.at[k],
            recv_sem=recv.at[slot],
            device_id=(target, yz),
            device_id_type=MESH,
        )

    def offer(*where):
        for k in range(1, half):
            share(*where, gx, peer(k), k).start()
        share(*where, gx, partner, 0).start()

    def relay(*where):
        for k in range(1, half):
            share(*where, peer(k), peer(k), k).wait_recv()
            share(*where, peer(k), partner, half + k).start()

    def collect(*where):
        share(*where, partner, partner, 0).wait_recv()
        for k in range(1, half):
            share(*where, lax.rem(partner + 2 * k, n_gx), partner, half + k).wait_recv()

    def release(*where):
        share(*where, gx, partner, 0).wait_send()
        for k in range(1, half):
            share(*where, gx, peer(k), k).wait_send()
            share(*where, peer(k), partner, half + k).wait_send()

    maps = (gmap, map_send, map_recv)
    offer(*maps)

    for g in range(groups):
        tall[g, :nv] = unit
        tall[g, nv:] = jnp.zeros((nv, nv), F32)
        wide_state[g] = second_unit

    def hom_backward(i, carry):
        x = cells - 1 - i
        for g in range(groups):
            m = hom[g, x + 1] + mul(get(bt, g, x), split(wide_state[g]))
            resp[g, 0, x], resp[g, 1, x] = split(m)
            wide_state[g] = m
            now = split(
                jnp.concatenate([tall[g, :nv], omega[g, x] + tall[g, nv:]], axis=0)
            )
            put(gain, g, x, split(mul(now, get(vt, g, x))))
            tall[g] = mul(now, get(ft, g, x))
        return carry

    loop(cells, hom_backward, 0)

    edge = cells - chunk
    block = next(c for c in (12, 6, 4, 3, 2, 1) if cells % c == 0)

    def weight(g, x):
        kind = cat[x][g : g + 1]
        return jnp.where(kind == 0, 1.0, jnp.where(kind == 2, 0.5, 0.0))

    def slope(g, x):
        if g == 0:
            return 8.0 * res[x, 1] + low[g, x] - high[g, x]
        return low[g, x] + high[g, x] - 8.0 * res[x, 0]

    def arrive(g, c):
        @pl.when(has_low)
        def _():
            halo(0, g, c).wait_recv()

        @pl.when(has_high)
        def _():
            halo(1, g, c).wait_recv()

    def local_forward(g, first, count, gather):
        xs = range(first, first + count)
        flux_in = [mul(held(g, 0), split(slope(g, x))) for x in xs]
        forces = [split(weight(g, x) * (res[x, g] + f)) for x, f in zip(xs, flux_in)]
        if gather:
            total = acc[g]
            for x, force in zip(xs, forces):
                total = total + mul(get(gain, g, x), force)
            acc[g] = total
        for x, force in zip(xs, forces):
            cs[g, x] = mul(get(vt, g, x), force)

    def parcel(g, target):
        return pltpu.make_async_remote_copy(
            src_ref=given.at[g, target],
            dst_ref=taken.at[g, gx],
            send_sem=vec_send.at[g, target],
            recv_sem=vec_recv.at[g, gx],
            device_id=(target, yz),
            device_id_type=MESH,
        )

    def receive(g, source):
        pltpu.make_async_remote_copy(
            src_ref=given.at[g, source],
            dst_ref=taken.at[g, source],
            send_sem=vec_send.at[g, source],
            recv_sem=vec_recv.at[g, source],
            device_id=(source, yz),
            device_id_type=MESH,
        ).wait_recv()

    def dispatch(g):
        ah, al = split(acc[g])
        for t in range(n_gx // 4):
            zh = send_map[g, 0, 4 * t : 4 * t + 4].reshape(4 * nv, 2 * nv)
            zl = send_map[g, 1, 4 * t : 4 * t + 4].reshape(4 * nv, 2 * nv)
            given[g, 4 * t : 4 * t + 4] = mul((zh, zl), (ah, al)).reshape(4, nv, nz)
        for k in range(1, n_gx):
            parcel(g, lax.rem(gx + k, n_gx)).start()

    def sweep():
        for g in range(groups):
            into_state[g] = cs[g, 0]

        def forward(i, carry):
            for g in range(groups):
                state = cs[g, i + 1] + mul(get(ft, g, i + 1), split(into_state[g]))
                into_state[g] = state
                cs[g, i + 1] = state
            return carry

        lax.fori_loop(0, cells - 1, forward, 0)

        def backward(i, carry):
            x = cells - 2 - i
            for g in range(groups):
                state = cs[g, x] + mul(get(bt, g, x), split(into_state[g]))
                into_state[g] = state
                cs[g, x] = state
            return carry

        lax.fori_loop(0, cells - 1, backward, 0)

    def finish(g):
        head = jnp.zeros((nv, nz), F32)
        tail = given[g, gx]
        for k in range(1, n_gx):
            j = lax.rem(gx + k, n_gx)
            receive(g, j)
            value = taken[g, j]
            head = head + jnp.where(j < gx, value, 0.0)
            tail = tail + jnp.where(j < gx, 0.0, value)
        both = split(jnp.concatenate([head, tail], axis=0))
        high_block = next(c for c in (4, 3, 2, 1) if cells % c == 0)
        for x in range(0, cells, high_block):
            maps_here = tuple(
                resp[g, n, x : x + high_block].reshape(high_block * nv, 2 * nv) for n in range(2)
            )
            fix = mul(maps_here, both).reshape(high_block, nv, nz)
            for k in range(high_block):
                value = cs[g, x + k] + fix[k]
                out[x + k, g] = jnp.where(cat[x + k][g : g + 1] != 1, value, 0.0)

    for g in range(groups):
        acc[g] = jnp.zeros((2 * nv, nz), F32)

    for c in range(pieces):
        arrive(0, c)
    for x in range(0, cells, block):
        local_forward(0, x, block, True)

    relay(*maps)
    collect(*maps)

    for g in range(groups):
        ahead[g, 0] = unit
        behind[g, n_gx] = unit
        mirror[g, 0] = unit

    def chains(t, carry):
        i = n_gx - 1 - t
        p_up = gmap[t, groups * nv :]
        grow = t > gx
        shrink = i < gx
        for g in range(groups):
            rows = slice(g * nv, (g + 1) * nv)
            step = mul(split(p_up[:, rows]), split(ahead[g, t]))
            ahead[g, t + 1] = jnp.where(grow, step, unit)
            step = mul(split(gmap[i, rows][:, nv:]), split(behind[g, i + 1]))
            behind[g, i] = jnp.where(shrink, step, unit)
            step = mul(split(mirror[g, t]), split(gmap[t, rows][:, nv:]))
            mirror[g, t + 1] = jnp.where(grow, step, unit)
        return carry

    loop(n_gx, chains, 0)

    for g in range(groups):
        rows = slice(g * nv, (g + 1) * nv)
        s_now = jnp.zeros((nv, nv), F32)
        inner = [mul(split(gmap[j, rows][:, :nv]), split(ahead[g, j])) for j in range(1, n_gx)]
        for j in range(1, n_gx):
            s_now = s_now + jnp.where(j > gx, mul(split(mirror[g, j]), split(inner[j - 1])), 0.0)
        zero = jnp.zeros((nv, nv), F32)
        qs = mul(split(gmap[gx, rows][:, nv:]), split(s_now))
        p_here = gmap[gx, groups * nv :][:, rows]
        sp = mul(split(s_now), split(p_here))
        left = jnp.concatenate([qs, unit], axis=1)
        for i in range(n_gx):
            m = mul(split(behind[g, i + 1]), split(left))
            m = jnp.where(i < gx, m, jnp.concatenate([ahead[g, i], zero], axis=1))
            m = jnp.where(gx == i, jnp.concatenate([s_now, zero], axis=1), m)
            send_map[g, 0, i], send_map[g, 1, i] = split(m)
        turn = split(
            jnp.concatenate(
                [first_unit, jnp.concatenate([sp, unit], axis=1)], axis=0
            )
        )
        high_block = next(c for c in (4, 3, 2, 1) if cells % c == 0)
        for x in range(0, cells, high_block):
            maps_here = tuple(
                resp[g, n, x : x + high_block].reshape(high_block * nv, 2 * nv) for n in range(2)
            )
            fixed = split(mul(maps_here, turn))
            for n in range(2):
                resp[g, n, x : x + high_block] = fixed[n].reshape(high_block, nv, 2 * nv)

    dispatch(0)

    last = groups - 1
    for n in range(chunk):
        x = edge + n
        fast[n, 0], fast[n, 1] = split(mul(get(gain, last, x), held(last, 0)))
        acc[last] += mul(get(gain, last, x), split(weight(last, x) * res[x, last]))

    for c in range(pieces - 1):
        arrive(last, c)
    for x in range(0, edge, min(edge, 9)):
        local_forward(last, x, min(9, edge - x), True)
    arrive(last, pieces - 1)
    for n in range(chunk):
        x = edge + n
        acc[last] += mul((fast[n, 0], fast[n, 1]), split(weight(last, x) * slope(last, x)))
    dispatch(last)
    local_forward(last, edge, chunk, False)
    sweep()
    for g in range(groups):
        finish(g)

    @pl.when(has_high)
    def _():
        for g in range(groups):
            for c in range(pieces):
                halo(0, g, c).wait_send()

    @pl.when(has_low)
    def _():
        for g in range(groups):
            for c in range(pieces):
                halo(1, g, c).wait_send()

    release(*maps)
    for g in range(groups):
        for k in range(1, n_gx):
            parcel(g, lax.rem(gx + k, n_gx)).wait_send()


def per_device(n_gx, n_yz, residual, inverses, upwind, downwind, flux_y, kinds, volume_category):
    cells, groups, nv, nz = residual.shape
    chunk = next(c for c in (3, 4, 2, 1) if cells % c == 0)
    pieces = cells // chunk
    hbm = pl.BlockSpec(memory_space=pltpu.HBM)
    operands = (residual, inverses, upwind, downwind, flux_y, volume_category, kinds)
    square = pltpu.VMEM((groups, cells, 2, nv, nv), BF16)
    wide = pltpu.VMEM((groups, cells, nv, nz), F32)
    return pl.pallas_call(
        functools.partial(kernel, n_gx, n_yz, chunk),
        out_shape=jax.ShapeDtypeStruct(residual.shape, F32),
        in_specs=[hbm] * 7,
        out_specs=pl.BlockSpec(memory_space=pltpu.VMEM),
        scratch_shapes=[pltpu.VMEM(a.shape, a.dtype) for a in operands[:-1]]
        + [
            pltpu.SMEM(kinds.shape, kinds.dtype),
            pltpu.VMEM((2, cells, nv, nz), F32),
            wide,
            wide,
            pltpu.VMEM((groups, 3, 2, nv, nv), BF16),
            square,
            square,
            square,
            pltpu.VMEM((groups, max(cells, n_gx) + 1, nv, 2 * nv), F32),
            pltpu.VMEM((groups, cells + 1, nv, nv), F32),
            pltpu.VMEM((groups, 2, nv, nv), BF16),
            pltpu.VMEM((groups, nv, 2 * nv), F32),
            pltpu.VMEM((groups, cells, 2, 2 * nv, nv), BF16),
            pltpu.VMEM((chunk, 2, 2 * nv, nv), BF16),
            pltpu.VMEM((groups, 2, cells, nv, 2 * nv), BF16),
            wide,
            pltpu.VMEM((groups, 2 * nv, nz), F32),
            pltpu.VMEM((n_gx, (groups + 1) * nv, 2 * nv), F32),
            pltpu.VMEM((groups, n_gx, nv, nz), F32),
            pltpu.VMEM((groups, n_gx, nv, nz), F32),
            pltpu.VMEM((groups, 2, n_gx, nv, 2 * nv), BF16),
            pltpu.VMEM((groups, n_gx + 1, nv, nv), F32),
            pltpu.VMEM((groups, n_gx + 1, nv, nv), F32),
            pltpu.VMEM((groups, n_gx + 1, nv, nv), F32),
            pltpu.VMEM((groups, nv, 2 * nv), F32),
            pltpu.VMEM((groups, 2 * nv, nv), F32),
            pltpu.VMEM((groups, nv, nz), F32),
            pltpu.SemaphoreType.DMA((7,)),
            pltpu.SemaphoreType.DMA((2, groups, pieces)),
            pltpu.SemaphoreType.DMA((2, groups, pieces)),
            pltpu.SemaphoreType.DMA((n_gx,)),
            pltpu.SemaphoreType.DMA((n_gx,)),
            pltpu.SemaphoreType.DMA((groups, n_gx)),
            pltpu.SemaphoreType.DMA((groups, n_gx)),
        ],
        compiler_params=pltpu.CompilerParams(
            collective_id=0, has_side_effects=True, vmem_limit_bytes=48 * 1024 * 1024
        ),
    )(*(pltpu.with_memory_space_constraint(a, pltpu.HBM) for a in operands))


def solution(mesh):
    in_specs = (
        P("gx", "yz", None, None),
        P("gx", "yz", None, None),
        P(),
        P(),
        P(),
        P("yz"),
        P("gx", "yz", None),
    )
    out_specs = P("gx", "yz", None, None)
    return jax.shard_map(
        functools.partial(per_device, mesh.shape["gx"], mesh.shape["yz"]),
        mesh=mesh,
        in_specs=in_specs,
        out_specs=out_specs,
        check_vma=False,
    )
```

```python
import functools

import jax
import jax.numpy as jnp
from jax import lax
from jax.experimental import pallas as pl
from jax.experimental.pallas import tpu as pltpu
from jax.sharding import PartitionSpec as P

MESH = pl.DeviceIdType.MESH
F32 = jnp.float32
BF16 = jnp.bfloat16


def split(a):
    high = a.astype(BF16)
    return high, (a - high.astype(F32)).astype(BF16)


def mul(a, b):
    ah, al = a
    bh, bl = b
    d = functools.partial(jnp.dot, preferred_element_type=F32)
    return d(ah, bh) + (d(ah, bl) + d(al, bh))


def loop(count, body, carry, unroll=1):
    unroll = unroll if count % unroll == 0 else 1

    def several(i, carry):
        for u in range(unroll):
            carry = body(i * unroll + u, carry)
        return carry

    return lax.fori_loop(0, count // unroll, several, carry)


def kernel(
    n_gx, n_yz, chunk, res_hbm, inv_hbm, up_hbm, down_hbm, flux_hbm, cat_hbm, kinds_hbm, out,
    res, inv, up, down, flux, cat, kinds,
    snd, low, high, table, vt, ft, bt, hom, omega, path, echo, gain, fast, resp, cs, acc, gmap, given, taken,
    send_map, ahead, behind, mirror, side, wide_state, tall, into_state,
    load_sem, halo_send, halo_recv, map_send, map_recv, vec_send, vec_recv,
):
    cells, groups, nv, nz = res.shape
    half = n_gx // 2
    pieces = cells // chunk
    gx = lax.axis_index("gx")
    yz = lax.axis_index("yz")
    partner = gx + 1 - 2 * lax.rem(gx, 2)
    has_low = yz > 0
    has_high = yz < n_yz - 1

    loads = [
        pltpu.make_async_copy(source, target, load_sem.at[n])
        for n, (source, target) in enumerate(
            (
                (res_hbm, res), (inv_hbm, inv), (up_hbm, up), (down_hbm, down),
                (flux_hbm, flux), (cat_hbm, cat), (kinds_hbm, kinds),
            )
        )
    ]
    for load in loads:
        load.start()

    def peer(k):
        return lax.rem(gx + 2 * k, n_gx)

    barrier = pltpu.get_barrier_semaphore()
    for k in range(1, n_gx):
        pl.semaphore_signal(
            barrier, inc=1, device_id=(lax.rem(gx + k, n_gx), yz), device_id_type=MESH
        )

    @pl.when(has_low)
    def _():
        pl.semaphore_signal(barrier, inc=1, device_id=(gx, yz - 1), device_id_type=MESH)

    @pl.when(has_high)
    def _():
        pl.semaphore_signal(barrier, inc=1, device_id=(gx, yz + 1), device_id_type=MESH)

    pl.semaphore_wait(barrier, n_gx - 1 + jnp.where(has_low, 1, 0) + jnp.where(has_high, 1, 0))

    def halo(direction, g, c):
        part = pl.ds(c * chunk, chunk)
        if direction == 0:
            src = snd.at[0, part] if g == 0 else res_hbm.at[part, 1]
            dst, where = low, yz + 1
        else:
            src = res_hbm.at[part, 0] if g == 0 else snd.at[1, part]
            dst, where = high, yz - 1
        return pltpu.make_async_remote_copy(
            src_ref=src,
            dst_ref=dst.at[g, part],
            send_sem=halo_send.at[direction, g, c],
            recv_sem=halo_recv.at[direction, g, c],
            device_id=(gx, where),
            device_id_type=MESH,
        )

    @pl.when(has_low)
    def _():
        for c in range(pieces):
            halo(1, 0, c).start()

    loads[0].wait()

    for c in range(pieces):
        for x in range(c * chunk, (c + 1) * chunk):
            snd[0, x] = res[x, 0] - 8.0 * res[x, 1]

        @pl.when(has_high)
        def _():
            halo(0, 0, c).start()

    @pl.when(has_high)
    def _():
        for c in range(pieces):
            halo(0, 1, c).start()

    for c in range(pieces):
        for x in range(c * chunk, (c + 1) * chunk):
            snd[1, x] = 8.0 * res[x, 0] - res[x, 1]

        @pl.when(has_low)
        def _():
            halo(1, 1, c).start()

    @pl.when(jnp.logical_not(has_low))
    def _():
        low[...] = jnp.zeros_like(low)

    @pl.when(jnp.logical_not(has_high))
    def _():
        high[...] = jnp.zeros_like(high)

    for load in loads[1:]:
        load.wait()

    for g in range(groups):
        kind = kinds[g]
        for n, block in enumerate((flux[kind] * (1.0 / 12.0), -up[kind], -down[kind])):
            table[g, n, 0], table[g, n, 1] = split(block.T)

    def held(g, n):
        return table[g, n, 0], table[g, n, 1]

    def put(ref, g, x, pair):
        ref[g, x, 0], ref[g, x, 1] = pair

    def get(ref, g, x):
        return ref[g, x, 0], ref[g, x, 1]

    def steps(x, carry):
        for g in range(groups):
            v = split(inv[x, g].T)
            put(vt, g, x, v)
            put(ft, g, x, split(mul(v, held(g, 1))))
            put(bt, g, x, split(mul(v, held(g, 2))))
        return carry

    loop(cells, steps, 0, 4)

    row = lax.broadcasted_iota(jnp.int32, (nv, 2 * nv), 0)
    col = lax.broadcasted_iota(jnp.int32, (nv, 2 * nv), 1)
    first_unit = (row == col).astype(F32)
    second_unit = (row + nv == col).astype(F32)
    square_row = lax.broadcasted_iota(jnp.int32, (nv, nv), 0)
    square_col = lax.broadcasted_iota(jnp.int32, (nv, nv), 1)
    unit = (square_row == square_col).astype(F32)
    for g in range(groups):
        hom[g, 0] = first_unit
        omega[g, 0] = unit
        path[g] = jnp.zeros((2, nv, nv), BF16)
        echo[g] = jnp.zeros((nv, 2 * nv), F32)

    def hom_forward(x, carry):
        for g in range(groups):
            onward = split(omega[g, x])
            ahead_of = tuple(
                jnp.concatenate([ft[g, x, n], path[g, n]], axis=0) for n in range(2)
            )
            both = mul(ahead_of, split(hom[g, x]))
            hom[g, x + 1] = both[:nv]
            echo[g] += both[nv:]
            omega[g, x + 1] = mul(onward, get(bt, g, x))
            path[g, 0], path[g, 1] = onward
        return carry

    loop(cells, hom_forward, 0)
    for g in range(groups):
        total = echo[g] + mul((path[g, 0], path[g, 1]), split(hom[g, cells]))
        gmap[gx, g * nv : (g + 1) * nv] = jnp.concatenate(
            [total[:, :nv], omega[g, cells]], axis=1
        )
    gmap[gx, groups * nv :] = jnp.concatenate(
        [hom[g, cells][:, :nv] for g in range(groups)], axis=1
    )

    def share(buffer, send, recv, slot, target, k):
        return pltpu.make_async_remote_copy(
            src_ref=buffer.at[slot],
            dst_ref=buffer.at[slot],
            send_sem=send.at[k],
            recv_sem=recv.at[slot],
            device_id=(target, yz),
            device_id_type=MESH,
        )

    def offer(*where):
        for k in range(1, half):
            share(*where, gx, peer(k), k).start()
        share(*where, gx, partner, 0).start()

    def relay(*where):
        for k in range(1, half):
            share(*where, peer(k), peer(k), k).wait_recv()
            share(*where, peer(k), partner, half + k).start()

    def collect(*where):
        share(*where, partner, partner, 0).wait_recv()
        for k in range(1, half):
            share(*where, lax.rem(partner + 2 * k, n_gx), partner, half + k).wait_recv()

    def release(*where):
        share(*where, gx, partner, 0).wait_send()
        for k in range(1, half):
            share(*where, gx, peer(k), k).wait_send()
            share(*where, peer(k), partner, half + k).wait_send()

    maps = (gmap, map_send, map_recv)
    offer(*maps)

    for g in range(groups):
        tall[g, :nv] = unit
        tall[g, nv:] = jnp.zeros((nv, nv), F32)
        wide_state[g] = second_unit

    def hom_backward(i, carry):
        x = cells - 1 - i
        for g in range(groups):
            m = hom[g, x + 1] + mul(get(bt, g, x), split(wide_state[g]))
            resp[g, 0, x], resp[g, 1, x] = split(m)
            wide_state[g] = m
            now = split(
                jnp.concatenate([tall[g, :nv], omega[g, x] + tall[g, nv:]], axis=0)
            )
            put(gain, g, x, split(mul(now, get(vt, g, x))))
            tall[g] = mul(now, get(ft, g, x))
        return carry

    loop(cells, hom_backward, 0)

    edge = cells - chunk
    block = next(c for c in (12, 6, 4, 3, 2, 1) if cells % c == 0)

    def weight(g, x):
        kind = cat[x][g : g + 1]
        return jnp.where(kind == 0, 1.0, jnp.where(kind == 2, 0.5, 0.0))

    def slope(g, x):
        if g == 0:
            return 8.0 * res[x, 1] + low[g, x] - high[g, x]
        return low[g, x] + high[g, x] - 8.0 * res[x, 0]

    def arrive(g, c):
        @pl.when(has_low)
        def _():
            halo(0, g, c).wait_recv()

        @pl.when(has_high)
        def _():
            halo(1, g, c).wait_recv()

    def local_forward(g, first, count, gather):
        xs = range(first, first + count)
        flux_in = [mul(held(g, 0), split(slope(g, x))) for x in xs]
        forces = [split(weight(g, x) * (res[x, g] + f)) for x, f in zip(xs, flux_in)]
        if gather:
            total = acc[g]
            for x, force in zip(xs, forces):
                total = total + mul(get(gain, g, x), force)
            acc[g] = total
        for x, force in zip(xs, forces):
            cs[g, x] = mul(get(vt, g, x), force)

    def parcel(g, target):
        return pltpu.make_async_remote_copy(
            src_ref=given.at[g, target],
            dst_ref=taken.at[g, gx],
            send_sem=vec_send.at[g, target],
            recv_sem=vec_recv.at[g, gx],
            device_id=(target, yz),
            device_id_type=MESH,
        )

    def receive(g, source):
        pltpu.make_async_remote_copy(
            src_ref=given.at[g, source],
            dst_ref=taken.at[g, source],
            send_sem=vec_send.at[g, source],
            recv_sem=vec_recv.at[g, source],
            device_id=(source, yz),
            device_id_type=MESH,
        ).wait_recv()

    def dispatch(g):
        ah, al = split(acc[g])
        for t in range(n_gx // 4):
            zh = send_map[g, 0, 4 * t : 4 * t + 4].reshape(4 * nv, 2 * nv)
            zl = send_map[g, 1, 4 * t : 4 * t + 4].reshape(4 * nv, 2 * nv)
            given[g, 4 * t : 4 * t + 4] = mul((zh, zl), (ah, al)).reshape(4, nv, nz)
        for k in range(1, n_gx):
            parcel(g, lax.rem(gx + k, n_gx)).start()

    def sweep_forward(g, first, count):
        def forward(i, carry):
            state = cs[g, i] + mul(get(ft, g, i), split(into_state[g]))
            into_state[g] = state
            cs[g, i] = state
            return carry

        lax.fori_loop(first, first + count, forward, 0)

    def sweep_backward():
        for g in range(groups):
            into_state[g] = jnp.zeros((nv, nz), F32)

        def backward(i, carry):
            x = cells - 1 - i
            for g in range(groups):
                state = cs[g, x] + mul(get(bt, g, x), split(into_state[g]))
                into_state[g] = state
                cs[g, x] = state
            return carry

        lax.fori_loop(0, cells, backward, 0)

    def finish(g):
        head = jnp.zeros((nv, nz), F32)
        tail = given[g, gx]
        for k in range(1, n_gx):
            j = lax.rem(gx + k, n_gx)
            receive(g, j)
            value = taken[g, j]
            head = head + jnp.where(j < gx, value, 0.0)
            tail = tail + jnp.where(j < gx, 0.0, value)
        both = split(jnp.concatenate([head, tail], axis=0))
        high_block = next(c for c in (4, 3, 2, 1) if cells % c == 0)
        for x in range(0, cells, high_block):
            maps_here = tuple(
                resp[g, n, x : x + high_block].reshape(high_block * nv, 2 * nv) for n in range(2)
            )
            fix = mul(maps_here, both).reshape(high_block, nv, nz)
            for k in range(high_block):
                value = cs[g, x + k] + fix[k]
                out[x + k, g] = jnp.where(cat[x + k][g : g + 1] != 1, value, 0.0)

    def turned(g):
        sp = side[g]
        turn = split(
            jnp.concatenate(
                [first_unit, jnp.concatenate([sp, unit], axis=1)], axis=0
            )
        )
        high_block = next(c for c in (4, 3, 2, 1) if cells % c == 0)
        for x in range(0, cells, high_block):
            maps_here = tuple(
                resp[g, n, x : x + high_block].reshape(high_block * nv, 2 * nv) for n in range(2)
            )
            fixed = split(mul(maps_here, turn))
            for n in range(2):
                resp[g, n, x : x + high_block] = fixed[n].reshape(high_block, nv, 2 * nv)

    for g in range(groups):
        acc[g] = jnp.zeros((2 * nv, nz), F32)

    for c in range(pieces):
        arrive(0, c)
    for x in range(0, cells, block):
        local_forward(0, x, block, True)

    last = groups - 1
    for n in range(chunk):
        x = edge + n
        fast[n, 0], fast[n, 1] = split(mul(get(gain, last, x), held(last, 0)))
        acc[last] += mul(get(gain, last, x), split(weight(last, x) * res[x, last]))
    for g in range(groups):
        into_state[g] = jnp.zeros((nv, nz), F32)
    sweep_forward(0, 0, cells)

    relay(*maps)
    first_wave = chunk if pieces > 1 else 0
    if first_wave:
        arrive(last, 0)
        local_forward(last, 0, chunk, True)
    collect(*maps)

    for g in range(groups):
        for t in range(2):
            ahead[g, t] = unit
            behind[g, n_gx - t] = unit
            mirror[g, t] = unit

    def chains(n, carry):
        t = n + 1
        i = n_gx - 1 - t
        p_up = gmap[t, groups * nv :]
        grow = t > gx
        shrink = i < gx
        for g in range(groups):
            rows = slice(g * nv, (g + 1) * nv)
            step = mul(split(p_up[:, rows]), split(ahead[g, t]))
            ahead[g, t + 1] = jnp.where(grow, step, unit)
            step = mul(split(gmap[i, rows][:, nv:]), split(behind[g, i + 1]))
            behind[g, i] = jnp.where(shrink, step, unit)
            step = mul(split(mirror[g, t]), split(gmap[t, rows][:, nv:]))
            mirror[g, t + 1] = jnp.where(grow, step, unit)
        return carry

    loop(n_gx - 2, chains, 0)

    for g in range(groups):
        rows = slice(g * nv, (g + 1) * nv)
        s_now = jnp.zeros((nv, nv), F32)
        inner = [mul(split(gmap[j, rows][:, :nv]), split(ahead[g, j])) for j in range(1, n_gx)]
        for j in range(1, n_gx):
            s_now = s_now + jnp.where(j > gx, mul(split(mirror[g, j]), split(inner[j - 1])), 0.0)
        zero = jnp.zeros((nv, nv), F32)
        qs = mul(split(gmap[gx, rows][:, nv:]), split(s_now))
        p_here = gmap[gx, groups * nv :][:, rows]
        sp = mul(split(s_now), split(p_here))
        left = jnp.concatenate([qs, unit], axis=1)
        for i in range(n_gx):
            m = mul(split(behind[g, i + 1]), split(left))
            m = jnp.where(i < gx, m, jnp.concatenate([ahead[g, i], zero], axis=1))
            m = jnp.where(gx == i, jnp.concatenate([s_now, zero], axis=1), m)
            send_map[g, 0, i], send_map[g, 1, i] = split(m)
        side[g] = sp

    dispatch(0)

    for c in range(1, pieces - 1):
        arrive(last, c)
    for x in range(first_wave, edge, 6):
        local_forward(last, x, min(6, edge - x), True)
    arrive(last, pieces - 1)
    for n in range(chunk):
        x = edge + n
        acc[last] += mul((fast[n, 0], fast[n, 1]), split(weight(last, x) * slope(last, x)))
    dispatch(last)
    local_forward(last, edge, chunk, False)
    for g in range(1, groups):
        sweep_forward(g, 0, cells)
    sweep_backward()
    for g in range(groups):
        turned(g)
    for g in range(groups):
        finish(g)

    @pl.when(has_high)
    def _():
        for g in range(groups):
            for c in range(pieces):
                halo(0, g, c).wait_send()

    @pl.when(has_low)
    def _():
        for g in range(groups):
            for c in range(pieces):
                halo(1, g, c).wait_send()

    release(*maps)
    for g in range(groups):
        for k in range(1, n_gx):
            parcel(g, lax.rem(gx + k, n_gx)).wait_send()


def per_device(n_gx, n_yz, residual, inverses, upwind, downwind, flux_y, kinds, volume_category):
    cells, groups, nv, nz = residual.shape
    chunk = next(c for c in (3, 4, 2, 1) if cells % c == 0)
    pieces = cells // chunk
    hbm = pl.BlockSpec(memory_space=pltpu.HBM)
    operands = (residual, inverses, upwind, downwind, flux_y, volume_category, kinds)
    square = pltpu.VMEM((groups, cells, 2, nv, nv), BF16)
    wide = pltpu.VMEM((groups, cells, nv, nz), F32)
    return pl.pallas_call(
        functools.partial(kernel, n_gx, n_yz, chunk),
        out_shape=jax.ShapeDtypeStruct(residual.shape, F32),
        in_specs=[hbm] * 7,
        out_specs=pl.BlockSpec(memory_space=pltpu.VMEM),
        scratch_shapes=[pltpu.VMEM(a.shape, a.dtype) for a in operands[:-1]]
        + [
            pltpu.SMEM(kinds.shape, kinds.dtype),
            pltpu.VMEM((2, cells, nv, nz), F32),
            wide,
            wide,
            pltpu.VMEM((groups, 3, 2, nv, nv), BF16),
            square,
            square,
            square,
            pltpu.VMEM((groups, max(cells, n_gx) + 1, nv, 2 * nv), F32),
            pltpu.VMEM((groups, cells + 1, nv, nv), F32),
            pltpu.VMEM((groups, 2, nv, nv), BF16),
            pltpu.VMEM((groups, nv, 2 * nv), F32),
            pltpu.VMEM((groups, cells, 2, 2 * nv, nv), BF16),
            pltpu.VMEM((chunk, 2, 2 * nv, nv), BF16),
            pltpu.VMEM((groups, 2, cells, nv, 2 * nv), BF16),
            wide,
            pltpu.VMEM((groups, 2 * nv, nz), F32),
            pltpu.VMEM((n_gx, (groups + 1) * nv, 2 * nv), F32),
            pltpu.VMEM((groups, n_gx, nv, nz), F32),
            pltpu.VMEM((groups, n_gx, nv, nz), F32),
            pltpu.VMEM((groups, 2, n_gx, nv, 2 * nv), BF16),
            pltpu.VMEM((groups, n_gx + 1, nv, nv), F32),
            pltpu.VMEM((groups, n_gx + 1, nv, nv), F32),
            pltpu.VMEM((groups, n_gx + 1, nv, nv), F32),
            pltpu.VMEM((groups, nv, nv), F32),
            pltpu.VMEM((groups, nv, 2 * nv), F32),
            pltpu.VMEM((groups, 2 * nv, nv), F32),
            pltpu.VMEM((groups, nv, nz), F32),
            pltpu.SemaphoreType.DMA((7,)),
            pltpu.SemaphoreType.DMA((2, groups, pieces)),
            pltpu.SemaphoreType.DMA((2, groups, pieces)),
            pltpu.SemaphoreType.DMA((n_gx,)),
            pltpu.SemaphoreType.DMA((n_gx,)),
            pltpu.SemaphoreType.DMA((groups, n_gx)),
            pltpu.SemaphoreType.DMA((groups, n_gx)),
        ],
        compiler_params=pltpu.CompilerParams(
            collective_id=0, has_side_effects=True, vmem_limit_bytes=48 * 1024 * 1024
        ),
    )(*(pltpu.with_memory_space_constraint(a, pltpu.HBM) for a in operands))


def solution(mesh):
    in_specs = (
        P("gx", "yz", None, None),
        P("gx", "yz", None, None),
        P(),
        P(),
        P(),
        P("yz"),
        P("gx", "yz", None),
    )
    out_specs = P("gx", "yz", None, None)
    return jax.shard_map(
        functools.partial(per_device, mesh.shape["gx"], mesh.shape["yz"]),
        mesh=mesh,
        in_specs=in_specs,
        out_specs=out_specs,
        check_vma=False,
    )
```

```python
import functools

import jax
import jax.numpy as jnp
from jax import lax
from jax.experimental import pallas as pl
from jax.experimental.pallas import tpu as pltpu
from jax.sharding import PartitionSpec as P

MESH = pl.DeviceIdType.MESH
F32 = jnp.float32
BF16 = jnp.bfloat16


def split(a):
    high = a.astype(BF16)
    return high, (a - high.astype(F32)).astype(BF16)


def mul(a, b):
    ah, al = a
    bh, bl = b
    d = functools.partial(jnp.dot, preferred_element_type=F32)
    return d(ah, bh) + (d(ah, bl) + d(al, bh))


def loop(count, body, carry, unroll=1):
    unroll = unroll if count % unroll == 0 else 1

    def several(i, carry):
        for u in range(unroll):
            carry = body(i * unroll + u, carry)
        return carry

    return lax.fori_loop(0, count // unroll, several, carry)


def cuts(cells):
    small = cells // 6
    if small == 0:
        return ((0, cells),)
    middle = (cells - 2 * small) // 2
    bounds = (0, small, small + middle, cells - small, cells)
    return tuple((a, b - a) for a, b in zip(bounds, bounds[1:]))


def kernel(
    n_gx, n_yz, res_hbm, inv_hbm, up_hbm, down_hbm, flux_hbm, cat_hbm, kinds_hbm, out,
    res, inv, up, down, flux, cat, kinds,
    snd, low, high, table, vt, ft, bt, hom, omega, path, echo, gain, fast, resp, cs, acc, gmap, given, taken,
    send_map, ahead, behind, mirror, side, wide_state, tall, into_state,
    load_sem, halo_send, halo_recv, map_send, map_recv, vec_send, vec_recv, ready,
):
    cells, groups, nv, nz = res.shape
    half = n_gx // 2
    parts = cuts(cells)
    pieces = len(parts)
    edge, chunk = parts[-1]
    gx = lax.axis_index("gx")
    yz = lax.axis_index("yz")
    partner = gx + 1 - 2 * lax.rem(gx, 2)
    has_low = yz > 0
    has_high = yz < n_yz - 1

    loads = [
        pltpu.make_async_copy(source, target, load_sem.at[n])
        for n, (source, target) in enumerate(
            (
                (res_hbm, res), (inv_hbm, inv), (up_hbm, up), (down_hbm, down),
                (flux_hbm, flux), (cat_hbm, cat), (kinds_hbm, kinds),
            )
        )
    ]
    for load in loads:
        load.start()

    def peer(k):
        return lax.rem(gx + 2 * k, n_gx)

    barrier = pltpu.get_barrier_semaphore()
    bits = n_gx.bit_length() - 1
    near = [
        gx + (1 << k) * (1 - 2 * lax.rem(lax.div(gx, 1 << k), 2)) for k in range(bits)
    ]

    def hail(semaphore):
        for device in near:
            pl.semaphore_signal(
                semaphore, inc=1, device_id=(device, yz), device_id_type=MESH
            )

    hail(barrier)

    @pl.when(has_low)
    def _():
        pl.semaphore_signal(barrier, inc=1, device_id=(gx, yz - 1), device_id_type=MESH)

    @pl.when(has_high)
    def _():
        pl.semaphore_signal(barrier, inc=1, device_id=(gx, yz + 1), device_id_type=MESH)

    pl.semaphore_wait(barrier, bits + jnp.where(has_low, 1, 0) + jnp.where(has_high, 1, 0))

    def halo(direction, g, c):
        part = pl.ds(*parts[c])
        if direction == 0:
            src = snd.at[0, part] if g == 0 else res_hbm.at[part, 1]
            dst, where = low, yz + 1
        else:
            src = res_hbm.at[part, 0] if g == 0 else snd.at[1, part]
            dst, where = high, yz - 1
        return pltpu.make_async_remote_copy(
            src_ref=src,
            dst_ref=dst.at[g, part],
            send_sem=halo_send.at[direction, g, c],
            recv_sem=halo_recv.at[direction, g, c],
            device_id=(gx, where),
            device_id_type=MESH,
        )

    last = groups - 1

    def emit(up, down):
        @pl.when(has_high)
        def _():
            for g, c in up:
                halo(0, g, c).start()

        @pl.when(has_low)
        def _():
            for g, c in down:
                halo(1, g, c).start()

    every = range(pieces)
    emit([(last, 0)], [(0, c) for c in every])

    loads[0].wait()

    for c in every:
        for x in range(parts[c][0], sum(parts[c])):
            snd[0, x] = res[x, 0] - 8.0 * res[x, 1]
        emit([(0, c)], [])

    emit([(last, c) for c in every[1:]], [])
    for c in every:
        for x in range(parts[c][0], sum(parts[c])):
            snd[1, x] = 8.0 * res[x, 0] - res[x, 1]
        emit([], [(last, c)])

    @pl.when(jnp.logical_not(has_low))
    def _():
        low[...] = jnp.zeros_like(low)

    @pl.when(jnp.logical_not(has_high))
    def _():
        high[...] = jnp.zeros_like(high)

    for load in loads[1:]:
        load.wait()

    for g in range(groups):
        kind = kinds[g]
        for n, block in enumerate((flux[kind] * (1.0 / 12.0), -up[kind], -down[kind])):
            table[g, n, 0], table[g, n, 1] = split(block.T)

    def held(g, n):
        return table[g, n, 0], table[g, n, 1]

    def put(ref, g, x, pair):
        ref[g, x, 0], ref[g, x, 1] = pair

    def get(ref, g, x):
        return ref[g, x, 0], ref[g, x, 1]

    def steps(x, carry):
        for g in range(groups):
            v = split(inv[x, g].T)
            put(vt, g, x, v)
            put(ft, g, x, split(mul(v, held(g, 1))))
            put(bt, g, x, split(mul(v, held(g, 2))))
        return carry

    hail(ready.at[0])
    loop(cells, steps, 0, 4)
    pl.semaphore_wait(ready.at[0], bits)

    row = lax.broadcasted_iota(jnp.int32, (nv, 2 * nv), 0)
    col = lax.broadcasted_iota(jnp.int32, (nv, 2 * nv), 1)
    first_unit = (row == col).astype(F32)
    second_unit = (row + nv == col).astype(F32)
    square_row = lax.broadcasted_iota(jnp.int32, (nv, nv), 0)
    square_col = lax.broadcasted_iota(jnp.int32, (nv, nv), 1)
    unit = (square_row == square_col).astype(F32)
    for g in range(groups):
        hom[g, 0] = first_unit
        omega[g, 0] = unit
        path[g] = jnp.zeros((2, nv, nv), BF16)
        echo[g] = jnp.zeros((nv, 2 * nv), F32)

    def hom_forward(x, carry):
        for g in range(groups):
            onward = split(omega[g, x])
            ahead_of = tuple(
                jnp.concatenate([ft[g, x, n], path[g, n]], axis=0) for n in range(2)
            )
            both = mul(ahead_of, split(hom[g, x]))
            hom[g, x + 1] = both[:nv]
            echo[g] += both[nv:]
            omega[g, x + 1] = mul(onward, get(bt, g, x))
            path[g, 0], path[g, 1] = onward
        return carry

    loop(cells, hom_forward, 0)
    for g in range(groups):
        total = echo[g] + mul((path[g, 0], path[g, 1]), split(hom[g, cells]))
        gmap[gx, g * nv : (g + 1) * nv] = jnp.concatenate(
            [total[:, :nv], omega[g, cells]], axis=1
        )
    gmap[gx, groups * nv :] = jnp.concatenate(
        [hom[g, cells][:, :nv] for g in range(groups)], axis=1
    )

    def share(buffer, send, recv, slot, target, k):
        return pltpu.make_async_remote_copy(
            src_ref=buffer.at[slot],
            dst_ref=buffer.at[slot],
            send_sem=send.at[k],
            recv_sem=recv.at[slot],
            device_id=(target, yz),
            device_id_type=MESH,
        )

    def offer(*where):
        for k in range(1, half):
            share(*where, gx, peer(k), k).start()
        share(*where, gx, partner, 0).start()

    def relay(*where):
        for k in range(1, half):
            share(*where, peer(k), peer(k), k).wait_recv()
            share(*where, peer(k), partner, half + k).start()

    def collect(*where):
        share(*where, partner, partner, 0).wait_recv()
        for k in range(1, half):
            share(*where, lax.rem(partner + 2 * k, n_gx), partner, half + k).wait_recv()

    def release(*where):
        share(*where, gx, partner, 0).wait_send()
        for k in range(1, half):
            share(*where, gx, peer(k), k).wait_send()
            share(*where, peer(k), partner, half + k).wait_send()

    maps = (gmap, map_send, map_recv)
    for r in range(1, bits - 1):
        hail(ready.at[r])
        pl.semaphore_wait(ready.at[r], bits)
    offer(*maps)

    for g in range(groups):
        tall[g, :nv] = unit
        tall[g, nv:] = jnp.zeros((nv, nv), F32)
        wide_state[g] = second_unit

    def hom_backward(i, carry):
        x = cells - 1 - i
        for g in range(groups):
            m = hom[g, x + 1] + mul(get(bt, g, x), split(wide_state[g]))
            resp[g, 0, x], resp[g, 1, x] = split(m)
            wide_state[g] = m
            now = split(
                jnp.concatenate([tall[g, :nv], omega[g, x] + tall[g, nv:]], axis=0)
            )
            put(gain, g, x, split(mul(now, get(vt, g, x))))
            tall[g] = mul(now, get(ft, g, x))
        return carry

    loop(cells, hom_backward, 0)

    block = next(c for c in (12, 6, 4, 3, 2, 1) if cells % c == 0)

    def weight(g, x):
        kind = cat[x][g : g + 1]
        return jnp.where(kind == 0, 1.0, jnp.where(kind == 2, 0.5, 0.0))

    def slope(g, x):
        if g == 0:
            return 8.0 * res[x, 1] + low[g, x] - high[g, x]
        return low[g, x] + high[g, x] - 8.0 * res[x, 0]

    def arrive(g, c):
        @pl.when(has_low)
        def _():
            halo(0, g, c).wait_recv()

        @pl.when(has_high)
        def _():
            halo(1, g, c).wait_recv()

    def local_forward(g, first, count, gather):
        xs = range(first, first + count)
        flux_in = [mul(held(g, 0), split(slope(g, x))) for x in xs]
        forces = [split(weight(g, x) * (res[x, g] + f)) for x, f in zip(xs, flux_in)]
        if gather:
            total = acc[g]
            for x, force in zip(xs, forces):
                total = total + mul(get(gain, g, x), force)
            acc[g] = total
        for x, force in zip(xs, forces):
            cs[g, x] = mul(get(vt, g, x), force)

    def parcel(g, target):
        return pltpu.make_async_remote_copy(
            src_ref=given.at[g, target],
            dst_ref=taken.at[g, gx],
            send_sem=vec_send.at[g, target],
            recv_sem=vec_recv.at[g, gx],
            device_id=(target, yz),
            device_id_type=MESH,
        )

    def receive(g, source):
        pltpu.make_async_remote_copy(
            src_ref=given.at[g, source],
            dst_ref=taken.at[g, source],
            send_sem=vec_send.at[g, source],
            recv_sem=vec_recv.at[g, source],
            device_id=(source, yz),
            device_id_type=MESH,
        ).wait_recv()

    def dispatch(g):
        ah, al = split(acc[g])
        for t in range(n_gx // 4):
            zh = send_map[g, 0, 4 * t : 4 * t + 4].reshape(4 * nv, 2 * nv)
            zl = send_map[g, 1, 4 * t : 4 * t + 4].reshape(4 * nv, 2 * nv)
            given[g, 4 * t : 4 * t + 4] = mul((zh, zl), (ah, al)).reshape(4, nv, nz)
        for k in range(1, n_gx):
            parcel(g, lax.rem(gx + k, n_gx)).start()

    def sweep_forward(first, count):
        def forward(i, carry):
            for g in range(groups):
                state = cs[g, i] + mul(get(ft, g, i), split(into_state[g]))
                into_state[g] = state
                cs[g, i] = state
            return carry

        lax.fori_loop(first, first + count, forward, 0)

    def sweep_backward():
        for g in range(groups):
            into_state[g] = jnp.zeros((nv, nz), F32)

        def backward(i, carry):
            x = cells - 1 - i
            for g in range(groups):
                state = cs[g, x] + mul(get(bt, g, x), split(into_state[g]))
                into_state[g] = state
                cs[g, x] = state
            return carry

        lax.fori_loop(0, cells, backward, 0)

    def finish(g):
        head = jnp.zeros((nv, nz), F32)
        tail = given[g, gx]
        for k in range(1, n_gx):
            j = lax.rem(gx + k, n_gx)
            receive(g, j)
            value = taken[g, j]
            head = head + jnp.where(j < gx, value, 0.0)
            tail = tail + jnp.where(j < gx, 0.0, value)
        both = split(jnp.concatenate([head, tail], axis=0))
        high_block = next(c for c in (4, 3, 2, 1) if cells % c == 0)
        for x in range(0, cells, high_block):
            maps_here = tuple(
                resp[g, n, x : x + high_block].reshape(high_block * nv, 2 * nv) for n in range(2)
            )
            fix = mul(maps_here, both).reshape(high_block, nv, nz)
            for k in range(high_block):
                value = cs[g, x + k] + fix[k]
                out[x + k, g] = jnp.where(cat[x + k][g : g + 1] != 1, value, 0.0)

    def turned(g):
        sp = side[g]
        turn = split(
            jnp.concatenate(
                [first_unit, jnp.concatenate([sp, unit], axis=1)], axis=0
            )
        )
        high_block = next(c for c in (4, 3, 2, 1) if cells % c == 0)
        for x in range(0, cells, high_block):
            maps_here = tuple(
                resp[g, n, x : x + high_block].reshape(high_block * nv, 2 * nv) for n in range(2)
            )
            fixed = split(mul(maps_here, turn))
            for n in range(2):
                resp[g, n, x : x + high_block] = fixed[n].reshape(high_block, nv, 2 * nv)

    for g in range(groups):
        acc[g] = jnp.zeros((2 * nv, nz), F32)

    for n in range(chunk):
        x = edge + n
        fast[n, 0], fast[n, 1] = split(mul(get(gain, last, x), held(last, 0)))
        acc[last] += mul(get(gain, last, x), split(weight(last, x) * res[x, last]))

    for c in every:
        arrive(0, c)
    for x in range(0, cells, block):
        local_forward(0, x, block, True)

    relay(*maps)
    collect(*maps)

    for g in range(groups):
        for t in range(2):
            ahead[g, t] = unit
            behind[g, n_gx - t] = unit
            mirror[g, t] = unit

    def chains(n, carry):
        t = n + 1
        i = n_gx - 1 - t
        p_up = gmap[t, groups * nv :]
        grow = t > gx
        shrink = i < gx
        for g in range(groups):
            rows = slice(g * nv, (g + 1) * nv)
            step = mul(split(p_up[:, rows]), split(ahead[g, t]))
            ahead[g, t + 1] = jnp.where(grow, step, unit)
            step = mul(split(gmap[i, rows][:, nv:]), split(behind[g, i + 1]))
            behind[g, i] = jnp.where(shrink, step, unit)
            step = mul(split(mirror[g, t]), split(gmap[t, rows][:, nv:]))
            mirror[g, t + 1] = jnp.where(grow, step, unit)
        return carry

    loop(n_gx - 2, chains, 0)

    for g in range(groups):
        rows = slice(g * nv, (g + 1) * nv)
        s_now = jnp.zeros((nv, nv), F32)
        inner = [mul(split(gmap[j, rows][:, :nv]), split(ahead[g, j])) for j in range(1, n_gx)]
        for j in range(1, n_gx):
            s_now = s_now + jnp.where(j > gx, mul(split(mirror[g, j]), split(inner[j - 1])), 0.0)
        zero = jnp.zeros((nv, nv), F32)
        qs = mul(split(gmap[gx, rows][:, nv:]), split(s_now))
        p_here = gmap[gx, groups * nv :][:, rows]
        sp = mul(split(s_now), split(p_here))
        left = jnp.concatenate([qs, unit], axis=1)
        for i in range(n_gx):
            m = mul(split(behind[g, i + 1]), split(left))
            m = jnp.where(i < gx, m, jnp.concatenate([ahead[g, i], zero], axis=1))
            m = jnp.where(gx == i, jnp.concatenate([s_now, zero], axis=1), m)
            send_map[g, 0, i], send_map[g, 1, i] = split(m)
        side[g] = sp

    dispatch(0)

    for c in every[:-1]:
        arrive(last, c)
    for x in range(0, edge, 5):
        local_forward(last, x, min(5, edge - x), True)
    for g in range(groups):
        into_state[g] = jnp.zeros((nv, nz), F32)

    early = edge // 2
    sweep_forward(0, early)

    arrive(last, pieces - 1)
    for n in range(chunk):
        x = edge + n
        acc[last] += mul((fast[n, 0], fast[n, 1]), split(weight(last, x) * slope(last, x)))
    dispatch(last)
    local_forward(last, edge, chunk, False)

    sweep_forward(early, cells - early)
    sweep_backward()
    for g in range(groups):
        turned(g)
    for g in range(groups):
        finish(g)

    @pl.when(has_high)
    def _():
        for g in range(groups):
            for c in range(pieces):
                halo(0, g, c).wait_send()

    @pl.when(has_low)
    def _():
        for g in range(groups):
            for c in range(pieces):
                halo(1, g, c).wait_send()

    release(*maps)
    for g in range(groups):
        for k in range(1, n_gx):
            parcel(g, lax.rem(gx + k, n_gx)).wait_send()


def per_device(n_gx, n_yz, residual, inverses, upwind, downwind, flux_y, kinds, volume_category):
    cells, groups, nv, nz = residual.shape
    pieces = len(cuts(cells))
    chunk = cuts(cells)[-1][1]
    hbm = pl.BlockSpec(memory_space=pltpu.HBM)
    operands = (residual, inverses, upwind, downwind, flux_y, volume_category, kinds)
    square = pltpu.VMEM((groups, cells, 2, nv, nv), BF16)
    wide = pltpu.VMEM((groups, cells, nv, nz), F32)
    return pl.pallas_call(
        functools.partial(kernel, n_gx, n_yz),
        out_shape=jax.ShapeDtypeStruct(residual.shape, F32),
        in_specs=[hbm] * 7,
        out_specs=pl.BlockSpec(memory_space=pltpu.VMEM),
        scratch_shapes=[pltpu.VMEM(a.shape, a.dtype) for a in operands[:-1]]
        + [
            pltpu.SMEM(kinds.shape, kinds.dtype),
            pltpu.VMEM((2, cells, nv, nz), F32),
            wide,
            wide,
            pltpu.VMEM((groups, 3, 2, nv, nv), BF16),
            square,
            square,
            square,
            pltpu.VMEM((groups, max(cells, n_gx) + 1, nv, 2 * nv), F32),
            pltpu.VMEM((groups, cells + 1, nv, nv), F32),
            pltpu.VMEM((groups, 2, nv, nv), BF16),
            pltpu.VMEM((groups, nv, 2 * nv), F32),
            pltpu.VMEM((groups, cells, 2, 2 * nv, nv), BF16),
            pltpu.VMEM((chunk, 2, 2 * nv, nv), BF16),
            pltpu.VMEM((groups, 2, cells, nv, 2 * nv), BF16),
            wide,
            pltpu.VMEM((groups, 2 * nv, nz), F32),
            pltpu.VMEM((n_gx, (groups + 1) * nv, 2 * nv), F32),
            pltpu.VMEM((groups, n_gx, nv, nz), F32),
            pltpu.VMEM((groups, n_gx, nv, nz), F32),
            pltpu.VMEM((groups, 2, n_gx, nv, 2 * nv), BF16),
            pltpu.VMEM((groups, n_gx + 1, nv, nv), F32),
            pltpu.VMEM((groups, n_gx + 1, nv, nv), F32),
            pltpu.VMEM((groups, n_gx + 1, nv, nv), F32),
            pltpu.VMEM((groups, nv, nv), F32),
            pltpu.VMEM((groups, nv, 2 * nv), F32),
            pltpu.VMEM((groups, 2 * nv, nv), F32),
            pltpu.VMEM((groups, nv, nz), F32),
            pltpu.SemaphoreType.DMA((7,)),
            pltpu.SemaphoreType.DMA((2, groups, pieces)),
            pltpu.SemaphoreType.DMA((2, groups, pieces)),
            pltpu.SemaphoreType.DMA((n_gx,)),
            pltpu.SemaphoreType.DMA((n_gx,)),
            pltpu.SemaphoreType.DMA((groups, n_gx)),
            pltpu.SemaphoreType.DMA((groups, n_gx)),
            pltpu.SemaphoreType.REGULAR((max(n_gx.bit_length() - 2, 1),)),
        ],
        compiler_params=pltpu.CompilerParams(
            collective_id=0, has_side_effects=True, vmem_limit_bytes=48 * 1024 * 1024
        ),
    )(*(pltpu.with_memory_space_constraint(a, pltpu.HBM) for a in operands))


def solution(mesh):
    in_specs = (
        P("gx", "yz", None, None),
        P("gx", "yz", None, None),
        P(),
        P(),
        P(),
        P("yz"),
        P("gx", "yz", None),
    )
    out_specs = P("gx", "yz", None, None)
    return jax.shard_map(
        functools.partial(per_device, mesh.shape["gx"], mesh.shape["yz"]),
        mesh=mesh,
        in_specs=in_specs,
        out_specs=out_specs,
        check_vma=False,
    )
```

```python
import functools

import jax
import jax.numpy as jnp
from jax import lax
from jax.experimental import pallas as pl
from jax.experimental.pallas import tpu as pltpu
from jax.sharding import PartitionSpec as P

MESH = pl.DeviceIdType.MESH
F32 = jnp.float32
BF16 = jnp.bfloat16


def split(a):
    high = a.astype(BF16)
    return high, (a - high.astype(F32)).astype(BF16)


def mul(a, b):
    ah, al = a
    bh, bl = b
    d = functools.partial(jnp.dot, preferred_element_type=F32)
    return d(ah, bh) + (d(ah, bl) + d(al, bh))


def loop(count, body, carry, unroll=1):
    unroll = unroll if count % unroll == 0 else 1

    def several(i, carry):
        for u in range(unroll):
            carry = body(i * unroll + u, carry)
        return carry

    return lax.fori_loop(0, count // unroll, several, carry)


def cuts(cells):
    small = cells // 6
    if small == 0:
        return ((0, cells),)
    middle = (cells - 2 * small) // 2
    bounds = (0, small, small + middle, cells - small, cells)
    return tuple((a, b - a) for a, b in zip(bounds, bounds[1:]))


def kernel(
    n_gx, n_yz, res_hbm, inv_hbm, up_hbm, down_hbm, flux_hbm, cat_hbm, kinds_hbm, out,
    res, inv, up, down, flux, cat, kinds,
    snd, low, high, table, vt, ft, bt, hom, omega, path, echo, gain, fast, resp, cs, acc, gmap, given, taken,
    send_map, ahead, behind, mirror, side, wide_state, tall, into_state,
    load_sem, halo_send, halo_recv, map_send, map_recv, vec_send, vec_recv, ready,
):
    cells, groups, nv, nz = res.shape
    half = n_gx // 2
    parts = cuts(cells)
    pieces = len(parts)
    edge, chunk = parts[-1]
    gx = lax.axis_index("gx")
    yz = lax.axis_index("yz")
    partner = gx + 1 - 2 * lax.rem(gx, 2)
    has_low = yz > 0
    has_high = yz < n_yz - 1

    loads = [
        pltpu.make_async_copy(source, target, load_sem.at[n])
        for n, (source, target) in enumerate(
            (
                (res_hbm, res), (inv_hbm, inv), (up_hbm, up), (down_hbm, down),
                (flux_hbm, flux), (cat_hbm, cat), (kinds_hbm, kinds),
            )
        )
    ]
    for load in loads:
        load.start()

    def peer(k):
        return lax.rem(gx + 2 * k, n_gx)

    barrier = pltpu.get_barrier_semaphore()
    bits = n_gx.bit_length() - 1
    near = [
        gx + (1 << k) * (1 - 2 * lax.rem(lax.div(gx, 1 << k), 2)) for k in range(bits)
    ]

    def hail(semaphore):
        for device in near:
            pl.semaphore_signal(
                semaphore, inc=1, device_id=(device, yz), device_id_type=MESH
            )

    hail(barrier)

    @pl.when(has_low)
    def _():
        pl.semaphore_signal(barrier, inc=1, device_id=(gx, yz - 1), device_id_type=MESH)

    @pl.when(has_high)
    def _():
        pl.semaphore_signal(barrier, inc=1, device_id=(gx, yz + 1), device_id_type=MESH)

    pl.semaphore_wait(barrier, bits + jnp.where(has_low, 1, 0) + jnp.where(has_high, 1, 0))

    def halo(direction, g, c):
        part = pl.ds(*parts[c])
        if direction == 0:
            src = snd.at[0, part] if g == 0 else res_hbm.at[part, 1]
            dst, where = low, yz + 1
        else:
            src = res_hbm.at[part, 0] if g == 0 else snd.at[1, part]
            dst, where = high, yz - 1
        return pltpu.make_async_remote_copy(
            src_ref=src,
            dst_ref=dst.at[g, part],
            send_sem=halo_send.at[direction, g, c],
            recv_sem=halo_recv.at[direction, g, c],
            device_id=(gx, where),
            device_id_type=MESH,
        )

    last = groups - 1

    def emit(up, down):
        @pl.when(has_high)
        def _():
            for g, c in up:
                halo(0, g, c).start()

        @pl.when(has_low)
        def _():
            for g, c in down:
                halo(1, g, c).start()

    every = range(pieces)
    emit([(last, 0)], [(0, c) for c in every])

    loads[0].wait()

    for c in every:
        for x in range(parts[c][0], sum(parts[c])):
            snd[0, x] = res[x, 0] - 8.0 * res[x, 1]
        emit([(0, c)], [])

    emit([(last, c) for c in every[1:]], [])
    for c in every:
        for x in range(parts[c][0], sum(parts[c])):
            snd[1, x] = 8.0 * res[x, 0] - res[x, 1]
        emit([], [(last, c)])

    @pl.when(jnp.logical_not(has_low))
    def _():
        low[...] = jnp.zeros_like(low)

    @pl.when(jnp.logical_not(has_high))
    def _():
        high[...] = jnp.zeros_like(high)

    for load in loads[1:]:
        load.wait()

    for g in range(groups):
        kind = kinds[g]
        for n, block in enumerate((flux[kind] * (1.0 / 12.0), -up[kind], -down[kind])):
            table[g, n, 0], table[g, n, 1] = split(block.T)

    def held(g, n):
        return table[g, n, 0], table[g, n, 1]

    def put(ref, g, x, pair):
        ref[g, x, 0], ref[g, x, 1] = pair

    def get(ref, g, x):
        return ref[g, x, 0], ref[g, x, 1]

    def steps(x, carry):
        for g in range(groups):
            v = split(inv[x, g].T)
            put(vt, g, x, v)
            put(ft, g, x, split(mul(v, held(g, 1))))
            put(bt, g, x, split(mul(v, held(g, 2))))
        return carry

    hail(ready.at[0])
    loop(cells, steps, 0, 4)
    pl.semaphore_wait(ready.at[0], bits)

    row = lax.broadcasted_iota(jnp.int32, (nv, 2 * nv), 0)
    col = lax.broadcasted_iota(jnp.int32, (nv, 2 * nv), 1)
    first_unit = (row == col).astype(F32)
    second_unit = (row + nv == col).astype(F32)
    square_row = lax.broadcasted_iota(jnp.int32, (nv, nv), 0)
    square_col = lax.broadcasted_iota(jnp.int32, (nv, nv), 1)
    unit = (square_row == square_col).astype(F32)
    for g in range(groups):
        hom[g, 0] = first_unit
        omega[g, 0] = unit
        path[g] = jnp.zeros((2, nv, nv), BF16)
        echo[g] = jnp.zeros((nv, 2 * nv), F32)

    def hom_forward(x, carry):
        for g in range(groups):
            onward = split(omega[g, x])
            ahead_of = tuple(
                jnp.concatenate([ft[g, x, n], path[g, n]], axis=0) for n in range(2)
            )
            both = mul(ahead_of, split(hom[g, x]))
            hom[g, x + 1] = both[:nv]
            echo[g] += both[nv:]
            omega[g, x + 1] = mul(onward, get(bt, g, x))
            path[g, 0], path[g, 1] = onward
        return carry

    loop(cells, hom_forward, 0)
    for g in range(groups):
        total = echo[g] + mul((path[g, 0], path[g, 1]), split(hom[g, cells]))
        gmap[gx, g * nv : (g + 1) * nv] = jnp.concatenate(
            [total[:, :nv], omega[g, cells]], axis=1
        )
    gmap[gx, groups * nv :] = jnp.concatenate(
        [hom[g, cells][:, :nv] for g in range(groups)], axis=1
    )

    def share(buffer, send, recv, slot, target, k):
        return pltpu.make_async_remote_copy(
            src_ref=buffer.at[slot],
            dst_ref=buffer.at[slot],
            send_sem=send.at[k],
            recv_sem=recv.at[slot],
            device_id=(target, yz),
            device_id_type=MESH,
        )

    def offer(*where):
        for k in range(1, half):
            share(*where, gx, peer(k), k).start()
        share(*where, gx, partner, 0).start()

    def relay(*where):
        for k in range(1, half):
            share(*where, peer(k), peer(k), k).wait_recv()
            share(*where, peer(k), partner, half + k).start()

    def collect(*where):
        share(*where, partner, partner, 0).wait_recv()
        for k in range(1, half):
            share(*where, lax.rem(partner + 2 * k, n_gx), partner, half + k).wait_recv()

    def release(*where):
        share(*where, gx, partner, 0).wait_send()
        for k in range(1, half):
            share(*where, gx, peer(k), k).wait_send()
            share(*where, peer(k), partner, half + k).wait_send()

    maps = (gmap, map_send, map_recv)
    for r in range(1, bits - 1):
        hail(ready.at[r])
        pl.semaphore_wait(ready.at[r], bits)
    offer(*maps)

    for g in range(groups):
        tall[g, :nv] = unit
        tall[g, nv:] = jnp.zeros((nv, nv), F32)
        wide_state[g] = second_unit

    def hom_backward(i, carry):
        x = cells - 1 - i
        for g in range(groups):
            m = hom[g, x + 1] + mul(get(bt, g, x), split(wide_state[g]))
            resp[g, 0, x], resp[g, 1, x] = split(m)
            wide_state[g] = m
            now = split(
                jnp.concatenate([tall[g, :nv], omega[g, x] + tall[g, nv:]], axis=0)
            )
            put(gain, g, x, split(mul(now, get(vt, g, x))))
            tall[g] = mul(now, get(ft, g, x))
        return carry

    loop(cells, hom_backward, 0)

    block = next(c for c in (12, 6, 4, 3, 2, 1) if cells % c == 0)

    def weight(g, x):
        kind = cat[x][g : g + 1]
        return jnp.where(kind == 0, 1.0, jnp.where(kind == 2, 0.5, 0.0))

    def slope(g, x):
        if g == 0:
            return 8.0 * res[x, 1] + low[g, x] - high[g, x]
        return low[g, x] + high[g, x] - 8.0 * res[x, 0]

    def arrive(g, c):
        @pl.when(has_low)
        def _():
            halo(0, g, c).wait_recv()

        @pl.when(has_high)
        def _():
            halo(1, g, c).wait_recv()

    def local_forward(g, first, count, gather):
        xs = range(first, first + count)
        flux_in = [mul(held(g, 0), split(slope(g, x))) for x in xs]
        forces = [split(weight(g, x) * (res[x, g] + f)) for x, f in zip(xs, flux_in)]
        if gather:
            total = acc[g]
            for x, force in zip(xs, forces):
                total = total + mul(get(gain, g, x), force)
            acc[g] = total
        for x, force in zip(xs, forces):
            cs[g, x] = mul(get(vt, g, x), force)

    def parcel(g, target):
        return pltpu.make_async_remote_copy(
            src_ref=given.at[g, target],
            dst_ref=taken.at[g, gx],
            send_sem=vec_send.at[g, target],
            recv_sem=vec_recv.at[g, gx],
            device_id=(target, yz),
            device_id_type=MESH,
        )

    def receive(g, source):
        pltpu.make_async_remote_copy(
            src_ref=given.at[g, source],
            dst_ref=taken.at[g, source],
            send_sem=vec_send.at[g, source],
            recv_sem=vec_recv.at[g, source],
            device_id=(source, yz),
            device_id_type=MESH,
        ).wait_recv()

    def dispatch(g):
        ah, al = split(acc[g])
        for t in range(n_gx // 4):
            zh = send_map[g, 0, 4 * t : 4 * t + 4].reshape(4 * nv, 2 * nv)
            zl = send_map[g, 1, 4 * t : 4 * t + 4].reshape(4 * nv, 2 * nv)
            given[g, 4 * t : 4 * t + 4] = mul((zh, zl), (ah, al)).reshape(4, nv, nz)
        for k in range(1, n_gx):
            parcel(g, lax.rem(gx + k, n_gx)).start()

    def sweep_forward(first, count):
        def forward(i, carry):
            for g in range(groups):
                state = cs[g, i] + mul(get(ft, g, i), split(into_state[g]))
                into_state[g] = state
                cs[g, i] = state
            return carry

        lax.fori_loop(first, first + count, forward, 0)

    def sweep_backward():
        for g in range(groups):
            into_state[g] = jnp.zeros((nv, nz), F32)

        def backward(i, carry):
            x = cells - 1 - i
            for g in range(groups):
                state = cs[g, x] + mul(get(bt, g, x), split(into_state[g]))
                into_state[g] = state
                cs[g, x] = state
            return carry

        lax.fori_loop(0, cells, backward, 0)

    def finish(g):
        head = jnp.zeros((nv, nz), F32)
        tail = given[g, gx]
        for k in range(1, n_gx):
            j = lax.rem(gx + k, n_gx)
            receive(g, j)
            value = taken[g, j]
            head = head + jnp.where(j < gx, value, 0.0)
            tail = tail + jnp.where(j < gx, 0.0, value)
        both = split(jnp.concatenate([head, tail], axis=0))
        high_block = next(c for c in (4, 3, 2, 1) if cells % c == 0)
        for x in range(0, cells, high_block):
            maps_here = tuple(
                resp[g, n, x : x + high_block].reshape(high_block * nv, 2 * nv) for n in range(2)
            )
            fix = mul(maps_here, both).reshape(high_block, nv, nz)
            for k in range(high_block):
                value = cs[g, x + k] + fix[k]
                out[x + k, g] = jnp.where(cat[x + k][g : g + 1] != 1, value, 0.0)

    def turned(g):
        sp = side[g]
        turn = split(
            jnp.concatenate(
                [first_unit, jnp.concatenate([sp, unit], axis=1)], axis=0
            )
        )
        high_block = next(c for c in (4, 3, 2, 1) if cells % c == 0)
        for x in range(0, cells, high_block):
            maps_here = tuple(
                resp[g, n, x : x + high_block].reshape(high_block * nv, 2 * nv) for n in range(2)
            )
            fixed = split(mul(maps_here, turn))
            for n in range(2):
                resp[g, n, x : x + high_block] = fixed[n].reshape(high_block, nv, 2 * nv)

    for g in range(groups):
        acc[g] = jnp.zeros((2 * nv, nz), F32)

    for n in range(chunk):
        x = edge + n
        fast[n, 0], fast[n, 1] = split(mul(get(gain, last, x), held(last, 0)))
        acc[last] += mul(get(gain, last, x), split(weight(last, x) * res[x, last]))

    relay(*maps)
    for c in every:
        arrive(0, c)
    for x in range(0, cells, block):
        local_forward(0, x, block, True)
    collect(*maps)

    for g in range(groups):
        for t in range(2):
            ahead[g, t] = unit
            behind[g, n_gx - t] = unit
            mirror[g, t] = unit

    def chains(n, carry):
        t = n + 1
        i = n_gx - 1 - t
        p_up = gmap[t, groups * nv :]
        grow = t > gx
        shrink = i < gx
        for g in range(groups):
            rows = slice(g * nv, (g + 1) * nv)
            step = mul(split(p_up[:, rows]), split(ahead[g, t]))
            ahead[g, t + 1] = jnp.where(grow, step, unit)
            step = mul(split(gmap[i, rows][:, nv:]), split(behind[g, i + 1]))
            behind[g, i] = jnp.where(shrink, step, unit)
            step = mul(split(mirror[g, t]), split(gmap[t, rows][:, nv:]))
            mirror[g, t + 1] = jnp.where(grow, step, unit)
        return carry

    loop(n_gx - 2, chains, 0)

    for g in range(groups):
        rows = slice(g * nv, (g + 1) * nv)
        s_now = jnp.zeros((nv, nv), F32)
        inner = [mul(split(gmap[j, rows][:, :nv]), split(ahead[g, j])) for j in range(1, n_gx)]
        for j in range(1, n_gx):
            s_now = s_now + jnp.where(j > gx, mul(split(mirror[g, j]), split(inner[j - 1])), 0.0)
        zero = jnp.zeros((nv, nv), F32)
        qs = mul(split(gmap[gx, rows][:, nv:]), split(s_now))
        p_here = gmap[gx, groups * nv :][:, rows]
        sp = mul(split(s_now), split(p_here))
        left = jnp.concatenate([qs, unit], axis=1)
        for i in range(n_gx):
            m = mul(split(behind[g, i + 1]), split(left))
            m = jnp.where(i < gx, m, jnp.concatenate([ahead[g, i], zero], axis=1))
            m = jnp.where(gx == i, jnp.concatenate([s_now, zero], axis=1), m)
            send_map[g, 0, i], send_map[g, 1, i] = split(m)
        side[g] = sp

    dispatch(0)

    for c in every[:-1]:
        arrive(last, c)
    for x in range(0, edge, 5):
        local_forward(last, x, min(5, edge - x), True)
    for g in range(groups):
        into_state[g] = jnp.zeros((nv, nz), F32)

    early = 0


    arrive(last, pieces - 1)
    for n in range(chunk):
        x = edge + n
        acc[last] += mul((fast[n, 0], fast[n, 1]), split(weight(last, x) * slope(last, x)))
    dispatch(last)
    local_forward(last, edge, chunk, False)

    sweep_forward(early, cells - early)
    sweep_backward()
    for g in range(groups):
        turned(g)
    for g in range(groups):
        finish(g)

    @pl.when(has_high)
    def _():
        for g in range(groups):
            for c in range(pieces):
                halo(0, g, c).wait_send()

    @pl.when(has_low)
    def _():
        for g in range(groups):
            for c in range(pieces):
                halo(1, g, c).wait_send()

    release(*maps)
    for g in range(groups):
        for k in range(1, n_gx):
            parcel(g, lax.rem(gx + k, n_gx)).wait_send()


def per_device(n_gx, n_yz, residual, inverses, upwind, downwind, flux_y, kinds, volume_category):
    cells, groups, nv, nz = residual.shape
    pieces = len(cuts(cells))
    chunk = cuts(cells)[-1][1]
    hbm = pl.BlockSpec(memory_space=pltpu.HBM)
    operands = (residual, inverses, upwind, downwind, flux_y, volume_category, kinds)
    square = pltpu.VMEM((groups, cells, 2, nv, nv), BF16)
    wide = pltpu.VMEM((groups, cells, nv, nz), F32)
    return pl.pallas_call(
        functools.partial(kernel, n_gx, n_yz),
        out_shape=jax.ShapeDtypeStruct(residual.shape, F32),
        in_specs=[hbm] * 7,
        out_specs=pl.BlockSpec(memory_space=pltpu.VMEM),
        scratch_shapes=[pltpu.VMEM(a.shape, a.dtype) for a in operands[:-1]]
        + [
            pltpu.SMEM(kinds.shape, kinds.dtype),
            pltpu.VMEM((2, cells, nv, nz), F32),
            wide,
            wide,
            pltpu.VMEM((groups, 3, 2, nv, nv), BF16),
            square,
            square,
            square,
            pltpu.VMEM((groups, max(cells, n_gx) + 1, nv, 2 * nv), F32),
            pltpu.VMEM((groups, cells + 1, nv, nv), F32),
            pltpu.VMEM((groups, 2, nv, nv), BF16),
            pltpu.VMEM((groups, nv, 2 * nv), F32),
            pltpu.VMEM((groups, cells, 2, 2 * nv, nv), BF16),
            pltpu.VMEM((chunk, 2, 2 * nv, nv), BF16),
            pltpu.VMEM((groups, 2, cells, nv, 2 * nv), BF16),
            wide,
            pltpu.VMEM((groups, 2 * nv, nz), F32),
            pltpu.VMEM((n_gx, (groups + 1) * nv, 2 * nv), F32),
            pltpu.VMEM((groups, n_gx, nv, nz), F32),
            pltpu.VMEM((groups, n_gx, nv, nz), F32),
            pltpu.VMEM((groups, 2, n_gx, nv, 2 * nv), BF16),
            pltpu.VMEM((groups, n_gx + 1, nv, nv), F32),
            pltpu.VMEM((groups, n_gx + 1, nv, nv), F32),
            pltpu.VMEM((groups, n_gx + 1, nv, nv), F32),
            pltpu.VMEM((groups, nv, nv), F32),
            pltpu.VMEM((groups, nv, 2 * nv), F32),
            pltpu.VMEM((groups, 2 * nv, nv), F32),
            pltpu.VMEM((groups, nv, nz), F32),
            pltpu.SemaphoreType.DMA((7,)),
            pltpu.SemaphoreType.DMA((2, groups, pieces)),
            pltpu.SemaphoreType.DMA((2, groups, pieces)),
            pltpu.SemaphoreType.DMA((n_gx,)),
            pltpu.SemaphoreType.DMA((n_gx,)),
            pltpu.SemaphoreType.DMA((groups, n_gx)),
            pltpu.SemaphoreType.DMA((groups, n_gx)),
            pltpu.SemaphoreType.REGULAR((max(n_gx.bit_length() - 2, 1),)),
        ],
        compiler_params=pltpu.CompilerParams(
            collective_id=0, has_side_effects=True, vmem_limit_bytes=48 * 1024 * 1024
        ),
    )(*(pltpu.with_memory_space_constraint(a, pltpu.HBM) for a in operands))


def solution(mesh):
    in_specs = (
        P("gx", "yz", None, None),
        P("gx", "yz", None, None),
        P(),
        P(),
        P(),
        P("yz"),
        P("gx", "yz", None),
    )
    out_specs = P("gx", "yz", None, None)
    return jax.shard_map(
        functools.partial(per_device, mesh.shape["gx"], mesh.shape["yz"]),
        mesh=mesh,
        in_specs=in_specs,
        out_specs=out_specs,
        check_vma=False,
    )
```

```python
import functools

import jax
import jax.numpy as jnp
from jax import lax
from jax.experimental import pallas as pl
from jax.experimental.pallas import tpu as pltpu
from jax.sharding import PartitionSpec as P

MESH = pl.DeviceIdType.MESH
F32 = jnp.float32
BF16 = jnp.bfloat16


def split(a):
    high = a.astype(BF16)
    return high, (a - high.astype(F32)).astype(BF16)


def mul(a, b):
    ah, al = a
    bh, bl = b
    d = functools.partial(jnp.dot, preferred_element_type=F32)
    return d(ah, bh) + (d(ah, bl) + d(al, bh))


def loop(count, body, carry, unroll=1):
    unroll = unroll if count % unroll == 0 else 1

    def several(i, carry):
        for u in range(unroll):
            carry = body(i * unroll + u, carry)
        return carry

    return lax.fori_loop(0, count // unroll, several, carry)


def cuts(cells):
    small = cells // 6
    if small == 0:
        return ((0, cells),)
    middle = (cells - 2 * small) // 2
    bounds = (0, small, small + middle, cells - small, cells)
    return tuple((a, b - a) for a, b in zip(bounds, bounds[1:]))


def kernel(
    n_gx, n_yz, res_hbm, inv_hbm, up_hbm, down_hbm, flux_hbm, cat_hbm, kinds_hbm, out,
    res, inv, up, down, flux, cat, kinds,
    snd, low, high, table, vt, ft, bt, hom, omega, path, echo, gain, fast, zfast, resp, cs, acc, gmap, given, taken,
    send_map, ahead, behind, mirror, side, wide_state, tall, into_state,
    load_sem, halo_send, halo_recv, map_send, map_recv, vec_send, vec_recv, ready,
):
    cells, groups, nv, nz = res.shape
    half = n_gx // 2
    parts = cuts(cells)
    pieces = len(parts)
    edge, chunk = parts[-1]
    gx = lax.axis_index("gx")
    yz = lax.axis_index("yz")
    partner = gx + 1 - 2 * lax.rem(gx, 2)
    has_low = yz > 0
    has_high = yz < n_yz - 1

    loads = [
        pltpu.make_async_copy(source, target, load_sem.at[n])
        for n, (source, target) in enumerate(
            (
                (res_hbm, res), (inv_hbm, inv), (up_hbm, up), (down_hbm, down),
                (flux_hbm, flux), (cat_hbm, cat), (kinds_hbm, kinds),
            )
        )
    ]
    for load in loads:
        load.start()

    def peer(k):
        return lax.rem(gx + 2 * k, n_gx)

    barrier = pltpu.get_barrier_semaphore()
    bits = n_gx.bit_length() - 1
    near = [
        gx + (1 << k) * (1 - 2 * lax.rem(lax.div(gx, 1 << k), 2)) for k in range(bits)
    ]

    def flip(k):
        return gx + sum(near[b] - gx for b in range(bits) if k >> b & 1)

    far_first = sorted(range(1, n_gx), key=lambda k: -bin(k >> 1).count("1"))

    def hail(semaphore):
        for device in near:
            pl.semaphore_signal(
                semaphore, inc=1, device_id=(device, yz), device_id_type=MESH
            )

    hail(barrier)

    @pl.when(has_low)
    def _():
        pl.semaphore_signal(barrier, inc=1, device_id=(gx, yz - 1), device_id_type=MESH)

    @pl.when(has_high)
    def _():
        pl.semaphore_signal(barrier, inc=1, device_id=(gx, yz + 1), device_id_type=MESH)

    pl.semaphore_wait(barrier, bits + jnp.where(has_low, 1, 0) + jnp.where(has_high, 1, 0))

    def halo(direction, g, c):
        part = pl.ds(*parts[c])
        if direction == 0:
            src = snd.at[0, part] if g == 0 else res_hbm.at[part, 1]
            dst, where = low, yz + 1
        else:
            src = res_hbm.at[part, 0] if g == 0 else snd.at[1, part]
            dst, where = high, yz - 1
        return pltpu.make_async_remote_copy(
            src_ref=src,
            dst_ref=dst.at[g, part],
            send_sem=halo_send.at[direction, g, c],
            recv_sem=halo_recv.at[direction, g, c],
            device_id=(gx, where),
            device_id_type=MESH,
        )

    last = groups - 1

    def emit(up, down):
        @pl.when(has_high)
        def _():
            for g, c in up:
                halo(0, g, c).start()

        @pl.when(has_low)
        def _():
            for g, c in down:
                halo(1, g, c).start()

    every = range(pieces)
    emit([(last, 0)], [(0, c) for c in every])

    loads[0].wait()

    for c in every:
        for x in range(parts[c][0], sum(parts[c])):
            snd[0, x] = res[x, 0] - 8.0 * res[x, 1]
        emit([(0, c)], [])

    emit([(last, c) for c in every[1:]], [])
    for c in every:
        for x in range(parts[c][0], sum(parts[c])):
            snd[1, x] = 8.0 * res[x, 0] - res[x, 1]
        emit([], [(last, c)])

    @pl.when(jnp.logical_not(has_low))
    def _():
        low[...] = jnp.zeros_like(low)

    @pl.when(jnp.logical_not(has_high))
    def _():
        high[...] = jnp.zeros_like(high)

    for load in loads[1:]:
        load.wait()

    for g in range(groups):
        kind = kinds[g]
        for n, block in enumerate((flux[kind] * (1.0 / 12.0), -up[kind], -down[kind])):
            table[g, n, 0], table[g, n, 1] = split(block.T)

    def held(g, n):
        return table[g, n, 0], table[g, n, 1]

    def put(ref, g, x, pair):
        ref[g, x, 0], ref[g, x, 1] = pair

    def get(ref, g, x):
        return ref[g, x, 0], ref[g, x, 1]

    def steps(x, carry):
        for g in range(groups):
            v = split(inv[x, g].T)
            put(vt, g, x, v)
            put(ft, g, x, split(mul(v, held(g, 1))))
            put(bt, g, x, split(mul(v, held(g, 2))))
        return carry

    hail(ready.at[0])
    loop(cells, steps, 0, 4)
    pl.semaphore_wait(ready.at[0], bits)

    row = lax.broadcasted_iota(jnp.int32, (nv, 2 * nv), 0)
    col = lax.broadcasted_iota(jnp.int32, (nv, 2 * nv), 1)
    first_unit = (row == col).astype(F32)
    second_unit = (row + nv == col).astype(F32)
    square_row = lax.broadcasted_iota(jnp.int32, (nv, nv), 0)
    square_col = lax.broadcasted_iota(jnp.int32, (nv, nv), 1)
    unit = (square_row == square_col).astype(F32)
    for g in range(groups):
        hom[g, 0] = first_unit
        omega[g, 0] = unit
        path[g] = jnp.zeros((2, nv, nv), BF16)
        echo[g] = jnp.zeros((nv, 2 * nv), F32)

    def hom_forward(x, carry):
        for g in range(groups):
            onward = split(omega[g, x])
            ahead_of = tuple(
                jnp.concatenate([ft[g, x, n], path[g, n]], axis=0) for n in range(2)
            )
            both = mul(ahead_of, split(hom[g, x]))
            hom[g, x + 1] = both[:nv]
            echo[g] += both[nv:]
            omega[g, x + 1] = mul(onward, get(bt, g, x))
            path[g, 0], path[g, 1] = onward
        return carry

    loop(cells, hom_forward, 0, 12)
    for g in range(groups):
        total = echo[g] + mul((path[g, 0], path[g, 1]), split(hom[g, cells]))
        gmap[gx, g * nv : (g + 1) * nv] = jnp.concatenate(
            [total[:, :nv], omega[g, cells]], axis=1
        )
    gmap[gx, groups * nv :] = jnp.concatenate(
        [hom[g, cells][:, :nv] for g in range(groups)], axis=1
    )

    def share(buffer, send, recv, slot, target, k):
        return pltpu.make_async_remote_copy(
            src_ref=buffer.at[slot],
            dst_ref=buffer.at[slot],
            send_sem=send.at[k],
            recv_sem=recv.at[slot],
            device_id=(target, yz),
            device_id_type=MESH,
        )

    def offer(*where):
        for k in range(1, half):
            share(*where, gx, peer(k), k).start()
        share(*where, gx, partner, 0).start()

    def relay(*where):
        for k in range(1, half):
            share(*where, peer(k), peer(k), k).wait_recv()
            share(*where, peer(k), partner, half + k).start()

    def collect(*where):
        share(*where, partner, partner, 0).wait_recv()
        for k in range(1, half):
            share(*where, lax.rem(partner + 2 * k, n_gx), partner, half + k).wait_recv()

    def release(*where):
        share(*where, gx, partner, 0).wait_send()
        for k in range(1, half):
            share(*where, gx, peer(k), k).wait_send()
            share(*where, peer(k), partner, half + k).wait_send()

    maps = (gmap, map_send, map_recv)
    for r in range(1, bits - 1):
        hail(ready.at[r])
        pl.semaphore_wait(ready.at[r], bits)
    offer(*maps)

    for g in range(groups):
        tall[g, :nv] = unit
        tall[g, nv:] = jnp.zeros((nv, nv), F32)
        wide_state[g] = second_unit

    def hom_backward(i, carry):
        x = cells - 1 - i
        for g in range(groups):
            m = hom[g, x + 1] + mul(get(bt, g, x), split(wide_state[g]))
            resp[g, 0, x], resp[g, 1, x] = split(m)
            wide_state[g] = m
            now = split(
                jnp.concatenate([tall[g, :nv], omega[g, x] + tall[g, nv:]], axis=0)
            )
            put(gain, g, x, split(mul(now, get(vt, g, x))))
            tall[g] = mul(now, get(ft, g, x))
        return carry

    loop(cells, hom_backward, 0, 4)

    block = next(c for c in (12, 6, 4, 3, 2, 1) if cells % c == 0)

    def weight(g, x):
        kind = cat[x][g : g + 1]
        return jnp.where(kind == 0, 1.0, jnp.where(kind == 2, 0.5, 0.0))

    def slope(g, x):
        if g == 0:
            return 8.0 * res[x, 1] + low[g, x] - high[g, x]
        return low[g, x] + high[g, x] - 8.0 * res[x, 0]

    def arrive(g, c):
        @pl.when(has_low)
        def _():
            halo(0, g, c).wait_recv()

        @pl.when(has_high)
        def _():
            halo(1, g, c).wait_recv()

    def local_forward(g, first, count, gather):
        xs = range(first, first + count)
        flux_in = [mul(held(g, 0), split(slope(g, x))) for x in xs]
        forces = [split(weight(g, x) * (res[x, g] + f)) for x, f in zip(xs, flux_in)]
        if gather:
            total = acc[g]
            for x, force in zip(xs, forces):
                total = total + mul(get(gain, g, x), force)
            acc[g] = total
        for x, force in zip(xs, forces):
            cs[g, x] = mul(get(vt, g, x), force)

    def parcel(g, target):
        return pltpu.make_async_remote_copy(
            src_ref=given.at[g, target],
            dst_ref=taken.at[g, gx],
            send_sem=vec_send.at[g, target],
            recv_sem=vec_recv.at[g, gx],
            device_id=(target, yz),
            device_id_type=MESH,
        )

    def receive(g, source):
        pltpu.make_async_remote_copy(
            src_ref=given.at[g, source],
            dst_ref=taken.at[g, source],
            send_sem=vec_send.at[g, source],
            recv_sem=vec_recv.at[g, source],
            device_id=(source, yz),
            device_id_type=MESH,
        ).wait_recv()

    def compose(g):
        ah, al = split(acc[g])
        for t in range(0, n_gx, 4):
            z = tuple(send_map[g, m, t : t + 4].reshape(4 * nv, 2 * nv) for m in range(2))
            given[g, t : t + 4] = mul(z, (ah, al)).reshape(4, nv, nz)

    def dispatch(g):
        for k in range(1, n_gx):
            parcel(g, lax.rem(gx + k, n_gx)).start()

    def sweep_forward(first, count):
        def forward(i, carry):
            for g in range(groups):
                state = cs[g, i] + mul(get(ft, g, i), split(into_state[g]))
                into_state[g] = state
                cs[g, i] = state
            return carry

        loop(count, lambda i, carry: forward(first + i, carry), 0, 4)

    def sweep_backward():
        for g in range(groups):
            into_state[g] = jnp.zeros((nv, nz), F32)

        def backward(i, carry):
            x = cells - 1 - i
            for g in range(groups):
                state = cs[g, x] + mul(get(bt, g, x), split(into_state[g]))
                into_state[g] = state
                cs[g, x] = state
            return carry

        loop(cells, backward, 0, 4)

    def finish(g):
        head = jnp.zeros((nv, nz), F32)
        tail = given[g, gx]
        for k in range(1, n_gx):
            j = lax.rem(gx + k, n_gx)
            receive(g, j)
            value = taken[g, j]
            head = head + jnp.where(j < gx, value, 0.0)
            tail = tail + jnp.where(j < gx, 0.0, value)
        both = split(jnp.concatenate([head, tail], axis=0))
        high_block = next(c for c in (4, 3, 2, 1) if cells % c == 0)
        for x in range(0, cells, high_block):
            maps_here = tuple(
                resp[g, n, x : x + high_block].reshape(high_block * nv, 2 * nv) for n in range(2)
            )
            fix = mul(maps_here, both).reshape(high_block, nv, nz)
            for k in range(high_block):
                value = cs[g, x + k] + fix[k]
                out[x + k, g] = jnp.where(cat[x + k][g : g + 1] != 1, value, 0.0)

    def turned(g):
        sp = side[g]
        turn = split(
            jnp.concatenate(
                [first_unit, jnp.concatenate([sp, unit], axis=1)], axis=0
            )
        )
        high_block = next(c for c in (4, 3, 2, 1) if cells % c == 0)
        for x in range(0, cells, high_block):
            maps_here = tuple(
                resp[g, n, x : x + high_block].reshape(high_block * nv, 2 * nv) for n in range(2)
            )
            fixed = split(mul(maps_here, turn))
            for n in range(2):
                resp[g, n, x : x + high_block] = fixed[n].reshape(high_block, nv, 2 * nv)

    for g in range(groups):
        acc[g] = jnp.zeros((2 * nv, nz), F32)

    for n in range(chunk):
        x = edge + n
        pair = split(mul(get(gain, last, x), held(last, 0)))
        for m in range(2):
            fast[m, :, n * nv : (n + 1) * nv] = pair[m]
        acc[last] += mul(get(gain, last, x), split(weight(last, x) * res[x, last]))

    relay(*maps)
    for c in every:
        arrive(0, c)
    for x in range(0, cells, block):
        local_forward(0, x, block, True)
    arrive(last, 0)
    local_forward(last, 0, parts[0][1] if pieces > 1 else 0, True)
    collect(*maps)

    for g in range(groups):
        for t in range(2):
            ahead[g, t] = unit
            behind[g, n_gx - t] = unit
            mirror[g, t] = unit

    def chains(n, carry):
        t = n + 1
        i = n_gx - 1 - t
        p_up = gmap[t, groups * nv :]
        grow = t > gx
        shrink = i < gx
        for g in range(groups):
            rows = slice(g * nv, (g + 1) * nv)
            step = mul(split(p_up[:, rows]), split(ahead[g, t]))
            ahead[g, t + 1] = jnp.where(grow, step, unit)
            step = mul(split(gmap[i, rows][:, nv:]), split(behind[g, i + 1]))
            behind[g, i] = jnp.where(shrink, step, unit)
            step = mul(split(mirror[g, t]), split(gmap[t, rows][:, nv:]))
            mirror[g, t + 1] = jnp.where(grow, step, unit)
        return carry

    loop(n_gx - 2, chains, 0, 6)

    for g in range(groups):
        rows = slice(g * nv, (g + 1) * nv)
        s_now = jnp.zeros((nv, nv), F32)
        inner = [mul(split(gmap[j, rows][:, :nv]), split(ahead[g, j])) for j in range(1, n_gx)]
        for j in range(1, n_gx):
            s_now = s_now + jnp.where(j > gx, mul(split(mirror[g, j]), split(inner[j - 1])), 0.0)
        zero = jnp.zeros((nv, nv), F32)
        qs = mul(split(gmap[gx, rows][:, nv:]), split(s_now))
        p_here = gmap[gx, groups * nv :][:, rows]
        sp = mul(split(s_now), split(p_here))
        left = jnp.concatenate([qs, unit], axis=1)
        for i in range(n_gx):
            m = mul(split(behind[g, i + 1]), split(left))
            m = jnp.where(i < gx, m, jnp.concatenate([ahead[g, i], zero], axis=1))
            m = jnp.where(gx == i, jnp.concatenate([s_now, zero], axis=1), m)
            send_map[g, 0, i], send_map[g, 1, i] = split(m)
        side[g] = sp

    compose(0)
    dispatch(0)

    for t in range(0, n_gx, 4):
        z = tuple(send_map[last, m, t : t + 4].reshape(4 * nv, 2 * nv) for m in range(2))
        quick = split(mul(z, (fast[0], fast[1])))
        for m in range(2):
            zfast[m, t : t + 4] = quick[m].reshape(4, nv, chunk * nv)
    for g in range(groups):
        turned(g)
    for g in range(groups):
        into_state[g] = jnp.zeros((nv, nz), F32)

    done = 0
    for c in every[1:-1]:
        arrive(last, c)
        local_forward(last, *parts[c], True)
        if c < pieces - 2 and True:
            sweep_forward(done, sum(parts[c]) - done)
            done = sum(parts[c])
    compose(last)

    arrive(last, pieces - 1)
    late = split(
        jnp.concatenate(
            [weight(last, x) * slope(last, x) for x in range(edge, cells)], axis=0
        )
    )
    for t in range(0, n_gx, 4):
        z = tuple(zfast[m, t : t + 4].reshape(4 * nv, chunk * nv) for m in range(2))
        given[last, t : t + 4] += mul(z, late).reshape(4, nv, nz)
    dispatch(last)
    local_forward(last, edge, chunk, False)

    sweep_forward(done, cells - done)
    sweep_backward()
    for g in range(groups):
        finish(g)

    @pl.when(has_high)
    def _():
        for g in range(groups):
            for c in range(pieces):
                halo(0, g, c).wait_send()

    @pl.when(has_low)
    def _():
        for g in range(groups):
            for c in range(pieces):
                halo(1, g, c).wait_send()

    release(*maps)
    for g in range(groups):
        for k in range(1, n_gx):
            parcel(g, lax.rem(gx + k, n_gx)).wait_send()


def per_device(n_gx, n_yz, residual, inverses, upwind, downwind, flux_y, kinds, volume_category):
    cells, groups, nv, nz = residual.shape
    pieces = len(cuts(cells))
    chunk = cuts(cells)[-1][1]
    hbm = pl.BlockSpec(memory_space=pltpu.HBM)
    operands = (residual, inverses, upwind, downwind, flux_y, volume_category, kinds)
    square = pltpu.VMEM((groups, cells, 2, nv, nv), BF16)
    wide = pltpu.VMEM((groups, cells, nv, nz), F32)
    return pl.pallas_call(
        functools.partial(kernel, n_gx, n_yz),
        out_shape=jax.ShapeDtypeStruct(residual.shape, F32),
        in_specs=[hbm] * 7,
        out_specs=pl.BlockSpec(memory_space=pltpu.VMEM),
        scratch_shapes=[pltpu.VMEM(a.shape, a.dtype) for a in operands[:-1]]
        + [
            pltpu.SMEM(kinds.shape, kinds.dtype),
            pltpu.VMEM((2, cells, nv, nz), F32),
            wide,
            wide,
            pltpu.VMEM((groups, 3, 2, nv, nv), BF16),
            square,
            square,
            square,
            pltpu.VMEM((groups, max(cells, n_gx) + 1, nv, 2 * nv), F32),
            pltpu.VMEM((groups, cells + 1, nv, nv), F32),
            pltpu.VMEM((groups, 2, nv, nv), BF16),
            pltpu.VMEM((groups, nv, 2 * nv), F32),
            pltpu.VMEM((groups, cells, 2, 2 * nv, nv), BF16),
            pltpu.VMEM((2, 2 * nv, chunk * nv), BF16),
            pltpu.VMEM((2, n_gx, nv, chunk * nv), BF16),
            pltpu.VMEM((groups, 2, cells, nv, 2 * nv), BF16),
            wide,
            pltpu.VMEM((groups, 2 * nv, nz), F32),
            pltpu.VMEM((n_gx, (groups + 1) * nv, 2 * nv), F32),
            pltpu.VMEM((groups, n_gx, nv, nz), F32),
            pltpu.VMEM((groups, n_gx, nv, nz), F32),
            pltpu.VMEM((groups, 2, n_gx, nv, 2 * nv), BF16),
            pltpu.VMEM((groups, n_gx + 1, nv, nv), F32),
            pltpu.VMEM((groups, n_gx + 1, nv, nv), F32),
            pltpu.VMEM((groups, n_gx + 1, nv, nv), F32),
            pltpu.VMEM((groups, nv, nv), F32),
            pltpu.VMEM((groups, nv, 2 * nv), F32),
            pltpu.VMEM((groups, 2 * nv, nv), F32),
            pltpu.VMEM((groups, nv, nz), F32),
            pltpu.SemaphoreType.DMA((7,)),
            pltpu.SemaphoreType.DMA((2, groups, pieces)),
            pltpu.SemaphoreType.DMA((2, groups, pieces)),
            pltpu.SemaphoreType.DMA((n_gx,)),
            pltpu.SemaphoreType.DMA((n_gx,)),
            pltpu.SemaphoreType.DMA((groups, n_gx)),
            pltpu.SemaphoreType.DMA((groups, n_gx)),
            pltpu.SemaphoreType.REGULAR((max(n_gx.bit_length() - 2, 1),)),
        ],
        compiler_params=pltpu.CompilerParams(
            collective_id=0, has_side_effects=True, vmem_limit_bytes=48 * 1024 * 1024
        ),
    )(*(pltpu.with_memory_space_constraint(a, pltpu.HBM) for a in operands))


def solution(mesh):
    in_specs = (
        P("gx", "yz", None, None),
        P("gx", "yz", None, None),
        P(),
        P(),
        P(),
        P("yz"),
        P("gx", "yz", None),
    )
    out_specs = P("gx", "yz", None, None)
    return jax.shard_map(
        functools.partial(per_device, mesh.shape["gx"], mesh.shape["yz"]),
        mesh=mesh,
        in_specs=in_specs,
        out_specs=out_specs,
        check_vma=False,
    )
```

```python
import functools

import jax
import jax.numpy as jnp
from jax import lax
from jax.experimental import pallas as pl
from jax.experimental.pallas import tpu as pltpu
from jax.sharding import PartitionSpec as P

MESH = pl.DeviceIdType.MESH
F32 = jnp.float32
BF16 = jnp.bfloat16


def split(a):
    high = a.astype(BF16)
    return high, (a - high.astype(F32)).astype(BF16)


def mul(a, b):
    ah, al = a
    bh, bl = b
    d = functools.partial(jnp.dot, preferred_element_type=F32)
    return d(ah, bh) + (d(ah, bl) + d(al, bh))


def loop(count, body, carry, unroll=1):
    unroll = unroll if count % unroll == 0 else 1

    def several(i, carry):
        for u in range(unroll):
            carry = body(i * unroll + u, carry)
        return carry

    return lax.fori_loop(0, count // unroll, several, carry)


def cuts(cells):
    small = cells // 6
    if small == 0:
        return ((0, cells),)
    middle = (cells - 2 * small) // 2
    bounds = (0, small, small + middle, cells - small, cells)
    return tuple((a, b - a) for a, b in zip(bounds, bounds[1:]))


def kernel(
    n_gx, n_yz, res_hbm, inv_hbm, up_hbm, down_hbm, flux_hbm, cat_hbm, kinds_hbm, out,
    res, inv, up, down, flux, cat, kinds,
    snd, low, high, table, vt, ft, bt, hom, omega, path, echo, gain, fast, zfast, resp, cs, acc, gmap, given, taken,
    send_map, ahead, behind, mirror, side, wide_state, tall, into_state,
    load_sem, halo_send, halo_recv, map_send, map_recv, vec_send, vec_recv, ready,
):
    cells, groups, nv, nz = res.shape
    half = n_gx // 2
    parts = cuts(cells)
    pieces = len(parts)
    edge, chunk = parts[-1]
    gx = lax.axis_index("gx")
    yz = lax.axis_index("yz")
    partner = gx + 1 - 2 * lax.rem(gx, 2)
    has_low = yz > 0
    has_high = yz < n_yz - 1

    loads = [
        pltpu.make_async_copy(source, target, load_sem.at[n])
        for n, (source, target) in enumerate(
            (
                (res_hbm, res), (inv_hbm, inv), (up_hbm, up), (down_hbm, down),
                (flux_hbm, flux), (cat_hbm, cat), (kinds_hbm, kinds),
            )
        )
    ]
    for load in loads:
        load.start()

    def peer(k):
        return lax.rem(gx + 2 * k, n_gx)

    barrier = pltpu.get_barrier_semaphore()
    bits = n_gx.bit_length() - 1
    near = [
        gx + (1 << k) * (1 - 2 * lax.rem(lax.div(gx, 1 << k), 2)) for k in range(bits)
    ]

    def flip(k):
        return gx + sum(near[b] - gx for b in range(bits) if k >> b & 1)

    far_first = sorted(range(1, n_gx), key=lambda k: -bin(k >> 1).count("1"))

    def hail(semaphore):
        for device in near:
            pl.semaphore_signal(
                semaphore, inc=1, device_id=(device, yz), device_id_type=MESH
            )

    hail(barrier)

    @pl.when(has_low)
    def _():
        pl.semaphore_signal(barrier, inc=1, device_id=(gx, yz - 1), device_id_type=MESH)

    @pl.when(has_high)
    def _():
        pl.semaphore_signal(barrier, inc=1, device_id=(gx, yz + 1), device_id_type=MESH)

    pl.semaphore_wait(barrier, bits + jnp.where(has_low, 1, 0) + jnp.where(has_high, 1, 0))

    def halo(direction, g, c):
        part = pl.ds(*parts[c])
        if direction == 0:
            src = snd.at[0, part] if g == 0 else res_hbm.at[part, 1]
            dst, where = low, yz + 1
        else:
            src = res_hbm.at[part, 0] if g == 0 else snd.at[1, part]
            dst, where = high, yz - 1
        return pltpu.make_async_remote_copy(
            src_ref=src,
            dst_ref=dst.at[g, part],
            send_sem=halo_send.at[direction, g, c],
            recv_sem=halo_recv.at[direction, g, c],
            device_id=(gx, where),
            device_id_type=MESH,
        )

    last = groups - 1

    def emit(up, down):
        @pl.when(has_high)
        def _():
            for g, c in up:
                halo(0, g, c).start()

        @pl.when(has_low)
        def _():
            for g, c in down:
                halo(1, g, c).start()

    every = range(pieces)
    emit([(last, 0)], [(0, c) for c in every])

    loads[0].wait()

    for c in every:
        for x in range(parts[c][0], sum(parts[c])):
            snd[0, x] = res[x, 0] - 8.0 * res[x, 1]
        emit([(0, c)], [])

    emit([(last, c) for c in every[1:]], [])
    for c in every:
        for x in range(parts[c][0], sum(parts[c])):
            snd[1, x] = 8.0 * res[x, 0] - res[x, 1]
        emit([], [(last, c)])

    @pl.when(jnp.logical_not(has_low))
    def _():
        low[...] = jnp.zeros_like(low)

    @pl.when(jnp.logical_not(has_high))
    def _():
        high[...] = jnp.zeros_like(high)

    for load in loads[1:]:
        load.wait()

    for g in range(groups):
        kind = kinds[g]
        for n, block in enumerate((flux[kind] * (1.0 / 12.0), -up[kind], -down[kind])):
            table[g, n, 0], table[g, n, 1] = split(block.T)

    def held(g, n):
        return table[g, n, 0], table[g, n, 1]

    def put(ref, g, x, pair):
        ref[g, x, 0], ref[g, x, 1] = pair

    def get(ref, g, x):
        return ref[g, x, 0], ref[g, x, 1]

    def steps(x, carry):
        for g in range(groups):
            v = split(inv[x, g].T)
            put(vt, g, x, v)
            put(ft, g, x, split(mul(v, held(g, 1))))
            put(bt, g, x, split(mul(v, held(g, 2))))
        return carry

    hail(ready.at[0])
    loop(cells, steps, 0, 4)
    pl.semaphore_wait(ready.at[0], bits)
    if bits > 2:
        hail(ready.at[1])

    row = lax.broadcasted_iota(jnp.int32, (nv, 2 * nv), 0)
    col = lax.broadcasted_iota(jnp.int32, (nv, 2 * nv), 1)
    first_unit = (row == col).astype(F32)
    second_unit = (row + nv == col).astype(F32)
    square_row = lax.broadcasted_iota(jnp.int32, (nv, nv), 0)
    square_col = lax.broadcasted_iota(jnp.int32, (nv, nv), 1)
    unit = (square_row == square_col).astype(F32)
    for g in range(groups):
        hom[g, 0] = first_unit
        omega[g, 0] = unit
        path[g] = jnp.zeros((2, nv, nv), BF16)
        echo[g] = jnp.zeros((nv, 2 * nv), F32)

    def hom_forward(x, carry):
        for g in range(groups):
            onward = split(omega[g, x])
            ahead_of = tuple(
                jnp.concatenate([ft[g, x, n], path[g, n]], axis=0) for n in range(2)
            )
            both = mul(ahead_of, split(hom[g, x]))
            hom[g, x + 1] = both[:nv]
            echo[g] += both[nv:]
            omega[g, x + 1] = mul(onward, get(bt, g, x))
            path[g, 0], path[g, 1] = onward
        return carry

    loop(cells, hom_forward, 0, 12)
    for g in range(groups):
        total = echo[g] + mul((path[g, 0], path[g, 1]), split(hom[g, cells]))
        gmap[gx, g * nv : (g + 1) * nv] = jnp.concatenate(
            [total[:, :nv], omega[g, cells]], axis=1
        )
    gmap[gx, groups * nv :] = jnp.concatenate(
        [hom[g, cells][:, :nv] for g in range(groups)], axis=1
    )

    def share(buffer, send, recv, slot, target, k):
        return pltpu.make_async_remote_copy(
            src_ref=buffer.at[slot],
            dst_ref=buffer.at[slot],
            send_sem=send.at[k],
            recv_sem=recv.at[slot],
            device_id=(target, yz),
            device_id_type=MESH,
        )

    def offer(*where):
        for k in range(1, half):
            share(*where, gx, peer(k), k).start()
        share(*where, gx, partner, 0).start()

    def relay(*where):
        for k in range(1, half):
            share(*where, peer(k), peer(k), k).wait_recv()
            share(*where, peer(k), partner, half + k).start()

    def collect(*where):
        share(*where, partner, partner, 0).wait_recv()
        for k in range(1, half):
            share(*where, lax.rem(partner + 2 * k, n_gx), partner, half + k).wait_recv()

    def release(*where):
        share(*where, gx, partner, 0).wait_send()
        for k in range(1, half):
            share(*where, gx, peer(k), k).wait_send()
            share(*where, peer(k), partner, half + k).wait_send()

    maps = (gmap, map_send, map_recv)
    for r in range(1, bits - 1):
        if r > 1:
            hail(ready.at[r])
        pl.semaphore_wait(ready.at[r], bits)
    offer(*maps)

    for g in range(groups):
        tall[g, :nv] = unit
        tall[g, nv:] = jnp.zeros((nv, nv), F32)
        wide_state[g] = second_unit

    def hom_backward(i, carry):
        x = cells - 1 - i
        for g in range(groups):
            m = hom[g, x + 1] + mul(get(bt, g, x), split(wide_state[g]))
            resp[g, 0, x], resp[g, 1, x] = split(m)
            wide_state[g] = m
            now = split(
                jnp.concatenate([tall[g, :nv], omega[g, x] + tall[g, nv:]], axis=0)
            )
            put(gain, g, x, split(mul(now, get(vt, g, x))))
            tall[g] = mul(now, get(ft, g, x))
        return carry

    loop(cells, hom_backward, 0, 4)

    block = next(c for c in (12, 6, 4, 3, 2, 1) if cells % c == 0)

    def weight(g, x):
        kind = cat[x][g : g + 1]
        return jnp.where(kind == 0, 1.0, jnp.where(kind == 2, 0.5, 0.0))

    def slope(g, x):
        if g == 0:
            return 8.0 * res[x, 1] + low[g, x] - high[g, x]
        return low[g, x] + high[g, x] - 8.0 * res[x, 0]

    def arrive(g, c):
        @pl.when(has_low)
        def _():
            halo(0, g, c).wait_recv()

        @pl.when(has_high)
        def _():
            halo(1, g, c).wait_recv()

    def local_forward(g, first, count, gather):
        xs = range(first, first + count)
        flux_in = [mul(held(g, 0), split(slope(g, x))) for x in xs]
        forces = [split(weight(g, x) * (res[x, g] + f)) for x, f in zip(xs, flux_in)]
        if gather:
            total = acc[g]
            for x, force in zip(xs, forces):
                total = total + mul(get(gain, g, x), force)
            acc[g] = total
        for x, force in zip(xs, forces):
            cs[g, x] = mul(get(vt, g, x), force)

    def parcel(g, target):
        return pltpu.make_async_remote_copy(
            src_ref=given.at[g, target],
            dst_ref=taken.at[g, gx],
            send_sem=vec_send.at[g, target],
            recv_sem=vec_recv.at[g, gx],
            device_id=(target, yz),
            device_id_type=MESH,
        )

    def receive(g, source):
        pltpu.make_async_remote_copy(
            src_ref=given.at[g, source],
            dst_ref=taken.at[g, source],
            send_sem=vec_send.at[g, source],
            recv_sem=vec_recv.at[g, source],
            device_id=(source, yz),
            device_id_type=MESH,
        ).wait_recv()

    def compose(g):
        ah, al = split(acc[g])
        for t in range(0, n_gx, 4):
            z = tuple(send_map[g, m, t : t + 4].reshape(4 * nv, 2 * nv) for m in range(2))
            given[g, t : t + 4] = mul(z, (ah, al)).reshape(4, nv, nz)

    def dispatch(g):
        for k in range(1, n_gx):
            parcel(g, lax.rem(gx + k, n_gx)).start()

    def sweep_forward(first, count):
        def forward(i, carry):
            for g in range(groups):
                state = cs[g, i] + mul(get(ft, g, i), split(into_state[g]))
                into_state[g] = state
                cs[g, i] = state
            return carry

        loop(count, lambda i, carry: forward(first + i, carry), 0, 4)

    def sweep_backward():
        for g in range(groups):
            into_state[g] = jnp.zeros((nv, nz), F32)

        def backward(i, carry):
            x = cells - 1 - i
            for g in range(groups):
                state = cs[g, x] + mul(get(bt, g, x), split(into_state[g]))
                into_state[g] = state
                cs[g, x] = state
            return carry

        loop(cells, backward, 0, 4)

    def finish(g):
        head = jnp.zeros((nv, nz), F32)
        tail = given[g, gx]
        for k in range(1, n_gx):
            j = lax.rem(gx + k, n_gx)
            receive(g, j)
            value = taken[g, j]
            head = head + jnp.where(j < gx, value, 0.0)
            tail = tail + jnp.where(j < gx, 0.0, value)
        both = split(jnp.concatenate([head, tail], axis=0))
        high_block = next(c for c in (4, 3, 2, 1) if cells % c == 0)
        for x in range(0, cells, high_block):
            maps_here = tuple(
                resp[g, n, x : x + high_block].reshape(high_block * nv, 2 * nv) for n in range(2)
            )
            fix = mul(maps_here, both).reshape(high_block, nv, nz)
            for k in range(high_block):
                value = cs[g, x + k] + fix[k]
                out[x + k, g] = jnp.where(cat[x + k][g : g + 1] != 1, value, 0.0)

    def turned(g):
        sp = side[g]
        turn = split(
            jnp.concatenate(
                [first_unit, jnp.concatenate([sp, unit], axis=1)], axis=0
            )
        )
        high_block = next(c for c in (4, 3, 2, 1) if cells % c == 0)
        for x in range(0, cells, high_block):
            maps_here = tuple(
                resp[g, n, x : x + high_block].reshape(high_block * nv, 2 * nv) for n in range(2)
            )
            fixed = split(mul(maps_here, turn))
            for n in range(2):
                resp[g, n, x : x + high_block] = fixed[n].reshape(high_block, nv, 2 * nv)

    for g in range(groups):
        acc[g] = jnp.zeros((2 * nv, nz), F32)

    for n in range(chunk):
        x = edge + n
        pair = split(mul(get(gain, last, x), held(last, 0)))
        for m in range(2):
            fast[m, :, n * nv : (n + 1) * nv] = pair[m]
        acc[last] += mul(get(gain, last, x), split(weight(last, x) * res[x, last]))

    relay(*maps)
    for c in every:
        arrive(0, c)
    for x in range(0, cells, block):
        local_forward(0, x, block, True)
    arrive(last, 0)
    local_forward(last, 0, parts[0][1] if pieces > 1 else 0, True)
    collect(*maps)

    for g in range(groups):
        for t in range(2):
            ahead[g, t] = unit
            behind[g, n_gx - t] = unit
            mirror[g, t] = unit

    def chains(n, carry):
        t = n + 1
        i = n_gx - 1 - t
        p_up = gmap[t, groups * nv :]
        grow = t > gx
        shrink = i < gx
        for g in range(groups):
            rows = slice(g * nv, (g + 1) * nv)
            step = mul(split(p_up[:, rows]), split(ahead[g, t]))
            ahead[g, t + 1] = jnp.where(grow, step, unit)
            step = mul(split(gmap[i, rows][:, nv:]), split(behind[g, i + 1]))
            behind[g, i] = jnp.where(shrink, step, unit)
            step = mul(split(mirror[g, t]), split(gmap[t, rows][:, nv:]))
            mirror[g, t + 1] = jnp.where(grow, step, unit)
        return carry

    loop(n_gx - 2, chains, 0, 6)

    for g in range(groups):
        rows = slice(g * nv, (g + 1) * nv)
        s_now = jnp.zeros((nv, nv), F32)
        inner = [mul(split(gmap[j, rows][:, :nv]), split(ahead[g, j])) for j in range(1, n_gx)]
        for j in range(1, n_gx):
            s_now = s_now + jnp.where(j > gx, mul(split(mirror[g, j]), split(inner[j - 1])), 0.0)
        zero = jnp.zeros((nv, nv), F32)
        qs = mul(split(gmap[gx, rows][:, nv:]), split(s_now))
        p_here = gmap[gx, groups * nv :][:, rows]
        sp = mul(split(s_now), split(p_here))
        left = jnp.concatenate([qs, unit], axis=1)
        for i in range(n_gx):
            m = mul(split(behind[g, i + 1]), split(left))
            m = jnp.where(i < gx, m, jnp.concatenate([ahead[g, i], zero], axis=1))
            m = jnp.where(gx == i, jnp.concatenate([s_now, zero], axis=1), m)
            send_map[g, 0, i], send_map[g, 1, i] = split(m)
        side[g] = sp

    compose(0)
    dispatch(0)

    for t in range(0, n_gx, 4):
        z = tuple(send_map[last, m, t : t + 4].reshape(4 * nv, 2 * nv) for m in range(2))
        quick = split(mul(z, (fast[0], fast[1])))
        for m in range(2):
            zfast[m, t : t + 4] = quick[m].reshape(4, nv, chunk * nv)
    for g in range(groups):
        turned(g)
    for g in range(groups):
        into_state[g] = jnp.zeros((nv, nz), F32)

    done = 0
    for c in every[1:-1]:
        arrive(last, c)
        local_forward(last, *parts[c], True)
        if c < pieces - 2 and True:
            sweep_forward(done, sum(parts[c]) - done)
            done = sum(parts[c])
    compose(last)

    arrive(last, pieces - 1)
    late = split(
        jnp.concatenate(
            [weight(last, x) * slope(last, x) for x in range(edge, cells)], axis=0
        )
    )
    for t in range(0, n_gx, 4):
        z = tuple(zfast[m, t : t + 4].reshape(4 * nv, chunk * nv) for m in range(2))
        given[last, t : t + 4] += mul(z, late).reshape(4, nv, nz)
    dispatch(last)
    local_forward(last, edge, chunk, False)

    sweep_forward(done, cells - done)
    sweep_backward()
    for g in range(groups):
        finish(g)

    @pl.when(has_high)
    def _():
        for g in range(groups):
            for c in range(pieces):
                halo(0, g, c).wait_send()

    @pl.when(has_low)
    def _():
        for g in range(groups):
            for c in range(pieces):
                halo(1, g, c).wait_send()

    release(*maps)
    for g in range(groups):
        for k in range(1, n_gx):
            parcel(g, lax.rem(gx + k, n_gx)).wait_send()


def per_device(n_gx, n_yz, residual, inverses, upwind, downwind, flux_y, kinds, volume_category):
    cells, groups, nv, nz = residual.shape
    pieces = len(cuts(cells))
    chunk = cuts(cells)[-1][1]
    hbm = pl.BlockSpec(memory_space=pltpu.HBM)
    operands = (residual, inverses, upwind, downwind, flux_y, volume_category, kinds)
    square = pltpu.VMEM((groups, cells, 2, nv, nv), BF16)
    wide = pltpu.VMEM((groups, cells, nv, nz), F32)
    return pl.pallas_call(
        functools.partial(kernel, n_gx, n_yz),
        out_shape=jax.ShapeDtypeStruct(residual.shape, F32),
        in_specs=[hbm] * 7,
        out_specs=pl.BlockSpec(memory_space=pltpu.VMEM),
        scratch_shapes=[pltpu.VMEM(a.shape, a.dtype) for a in operands[:-1]]
        + [
            pltpu.SMEM(kinds.shape, kinds.dtype),
            pltpu.VMEM((2, cells, nv, nz), F32),
            wide,
            wide,
            pltpu.VMEM((groups, 3, 2, nv, nv), BF16),
            square,
            square,
            square,
            pltpu.VMEM((groups, max(cells, n_gx) + 1, nv, 2 * nv), F32),
            pltpu.VMEM((groups, cells + 1, nv, nv), F32),
            pltpu.VMEM((groups, 2, nv, nv), BF16),
            pltpu.VMEM((groups, nv, 2 * nv), F32),
            pltpu.VMEM((groups, cells, 2, 2 * nv, nv), BF16),
            pltpu.VMEM((2, 2 * nv, chunk * nv), BF16),
            pltpu.VMEM((2, n_gx, nv, chunk * nv), BF16),
            pltpu.VMEM((groups, 2, cells, nv, 2 * nv), BF16),
            wide,
            pltpu.VMEM((groups, 2 * nv, nz), F32),
            pltpu.VMEM((n_gx, (groups + 1) * nv, 2 * nv), F32),
            pltpu.VMEM((groups, n_gx, nv, nz), F32),
            pltpu.VMEM((groups, n_gx, nv, nz), F32),
            pltpu.VMEM((groups, 2, n_gx, nv, 2 * nv), BF16),
            pltpu.VMEM((groups, n_gx + 1, nv, nv), F32),
            pltpu.VMEM((groups, n_gx + 1, nv, nv), F32),
            pltpu.VMEM((groups, n_gx + 1, nv, nv), F32),
            pltpu.VMEM((groups, nv, nv), F32),
            pltpu.VMEM((groups, nv, 2 * nv), F32),
            pltpu.VMEM((groups, 2 * nv, nv), F32),
            pltpu.VMEM((groups, nv, nz), F32),
            pltpu.SemaphoreType.DMA((7,)),
            pltpu.SemaphoreType.DMA((2, groups, pieces)),
            pltpu.SemaphoreType.DMA((2, groups, pieces)),
            pltpu.SemaphoreType.DMA((n_gx,)),
            pltpu.SemaphoreType.DMA((n_gx,)),
            pltpu.SemaphoreType.DMA((groups, n_gx)),
            pltpu.SemaphoreType.DMA((groups, n_gx)),
            pltpu.SemaphoreType.REGULAR((max(n_gx.bit_length() - 2, 1),)),
        ],
        compiler_params=pltpu.CompilerParams(
            collective_id=0, has_side_effects=True, vmem_limit_bytes=48 * 1024 * 1024
        ),
    )(*(pltpu.with_memory_space_constraint(a, pltpu.HBM) for a in operands))


def solution(mesh):
    in_specs = (
        P("gx", "yz", None, None),
        P("gx", "yz", None, None),
        P(),
        P(),
        P(),
        P("yz"),
        P("gx", "yz", None),
    )
    out_specs = P("gx", "yz", None, None)
    return jax.shard_map(
        functools.partial(per_device, mesh.shape["gx"], mesh.shape["yz"]),
        mesh=mesh,
        in_specs=in_specs,
        out_specs=out_specs,
        check_vma=False,
    )
```

```python
import functools

import jax
import jax.numpy as jnp
from jax import lax
from jax.experimental import pallas as pl
from jax.experimental.pallas import tpu as pltpu
from jax.sharding import PartitionSpec as P

MESH = pl.DeviceIdType.MESH
F32 = jnp.float32
BF16 = jnp.bfloat16


def split(a):
    high = a.astype(BF16)
    return high, (a - high.astype(F32)).astype(BF16)


def mul(a, b):
    ah, al = a
    bh, bl = b
    d = functools.partial(jnp.dot, preferred_element_type=F32)
    return d(ah, bh) + (d(ah, bl) + d(al, bh))


def loop(count, body, carry, unroll=1):
    unroll = unroll if count % unroll == 0 else 1

    def several(i, carry):
        for u in range(unroll):
            carry = body(i * unroll + u, carry)
        return carry

    return lax.fori_loop(0, count // unroll, several, carry)


def cuts(cells):
    small = cells // 6
    if small == 0:
        return ((0, cells),)
    first = (small + 1) // 2
    bounds = (0, first, cells // 2, cells - small, cells)
    return tuple((a, b - a) for a, b in zip(bounds, bounds[1:]))


def kernel(
    n_gx, n_yz, res_hbm, inv_hbm, up_hbm, down_hbm, flux_hbm, cat_hbm, kinds_hbm, out,
    res, inv, up, down, flux, cat, kinds,
    snd, low, high, table, vt, ft, bt, hom, omega, path, echo, gain, fast, zfast, resp, cs, acc, gmap, given, taken,
    send_map, ahead, behind, mirror, side, wide_state, tall, into_state,
    load_sem, halo_send, halo_recv, map_send, map_recv, vec_send, vec_recv, ready,
):
    cells, groups, nv, nz = res.shape
    half = n_gx // 2
    parts = cuts(cells)
    pieces = len(parts)
    edge, chunk = parts[-1]
    gx = lax.axis_index("gx")
    yz = lax.axis_index("yz")
    partner = gx + 1 - 2 * lax.rem(gx, 2)
    has_low = yz > 0
    has_high = yz < n_yz - 1

    loads = [
        pltpu.make_async_copy(source, target, load_sem.at[n])
        for n, (source, target) in enumerate(
            (
                (res_hbm, res), (inv_hbm, inv), (up_hbm, up), (down_hbm, down),
                (flux_hbm, flux), (cat_hbm, cat), (kinds_hbm, kinds),
            )
        )
    ]
    for load in loads:
        load.start()

    def peer(k):
        return lax.rem(gx + 2 * k, n_gx)

    barrier = pltpu.get_barrier_semaphore()
    bits = n_gx.bit_length() - 1
    near = [
        gx + (1 << k) * (1 - 2 * lax.rem(lax.div(gx, 1 << k), 2)) for k in range(bits)
    ]

    def flip(k):
        return gx + sum(near[b] - gx for b in range(bits) if k >> b & 1)

    far_first = sorted(range(1, n_gx), key=lambda k: -bin(k >> 1).count("1"))

    def hail(semaphore):
        for device in near:
            pl.semaphore_signal(
                semaphore, inc=1, device_id=(device, yz), device_id_type=MESH
            )

    hail(barrier)

    @pl.when(has_low)
    def _():
        pl.semaphore_signal(barrier, inc=1, device_id=(gx, yz - 1), device_id_type=MESH)

    @pl.when(has_high)
    def _():
        pl.semaphore_signal(barrier, inc=1, device_id=(gx, yz + 1), device_id_type=MESH)

    pl.semaphore_wait(barrier, bits + jnp.where(has_low, 1, 0) + jnp.where(has_high, 1, 0))

    def halo(direction, g, c):
        part = pl.ds(*parts[c])
        if direction == 0:
            src = snd.at[0, part] if g == 0 else res_hbm.at[part, 1]
            dst, where = low, yz + 1
        else:
            src = res_hbm.at[part, 0] if g == 0 else snd.at[1, part]
            dst, where = high, yz - 1
        return pltpu.make_async_remote_copy(
            src_ref=src,
            dst_ref=dst.at[g, part],
            send_sem=halo_send.at[direction, g, c],
            recv_sem=halo_recv.at[direction, g, c],
            device_id=(gx, where),
            device_id_type=MESH,
        )

    last = groups - 1

    def emit(up, down):
        @pl.when(has_high)
        def _():
            for g, c in up:
                halo(0, g, c).start()

        @pl.when(has_low)
        def _():
            for g, c in down:
                halo(1, g, c).start()

    every = range(pieces)
    emit([(last, 0)], [(0, c) for c in every])

    loads[0].wait()

    for c in every:
        for x in range(parts[c][0], sum(parts[c])):
            snd[0, x] = res[x, 0] - 8.0 * res[x, 1]
        emit([(0, c)], [])

    emit([(last, c) for c in every[1:]], [])
    for c in every:
        for x in range(parts[c][0], sum(parts[c])):
            snd[1, x] = 8.0 * res[x, 0] - res[x, 1]
        emit([], [(last, c)])

    @pl.when(jnp.logical_not(has_low))
    def _():
        low[...] = jnp.zeros_like(low)

    @pl.when(jnp.logical_not(has_high))
    def _():
        high[...] = jnp.zeros_like(high)

    for load in loads[1:]:
        load.wait()

    for g in range(groups):
        kind = kinds[g]
        for n, block in enumerate((flux[kind] * (1.0 / 12.0), -up[kind], -down[kind])):
            table[g, n, 0], table[g, n, 1] = split(block.T)

    def held(g, n):
        return table[g, n, 0], table[g, n, 1]

    def put(ref, g, x, pair):
        ref[g, x, 0], ref[g, x, 1] = pair

    def get(ref, g, x):
        return ref[g, x, 0], ref[g, x, 1]

    def steps(x, carry):
        for g in range(groups):
            v = split(inv[x, g].T)
            put(vt, g, x, v)
            put(ft, g, x, split(mul(v, held(g, 1))))
            put(bt, g, x, split(mul(v, held(g, 2))))
        return carry

    hail(ready.at[0])
    loop(cells, steps, 0, 4)
    pl.semaphore_wait(ready.at[0], bits)
    if bits > 2:
        hail(ready.at[1])

    row = lax.broadcasted_iota(jnp.int32, (nv, 2 * nv), 0)
    col = lax.broadcasted_iota(jnp.int32, (nv, 2 * nv), 1)
    first_unit = (row == col).astype(F32)
    second_unit = (row + nv == col).astype(F32)
    square_row = lax.broadcasted_iota(jnp.int32, (nv, nv), 0)
    square_col = lax.broadcasted_iota(jnp.int32, (nv, nv), 1)
    unit = (square_row == square_col).astype(F32)
    for g in range(groups):
        hom[g, 0] = first_unit
        omega[g, 0] = unit
        path[g] = jnp.zeros((2, nv, nv), BF16)
        echo[g] = jnp.zeros((nv, 2 * nv), F32)

    def hom_forward(x, carry):
        for g in range(groups):
            onward = split(omega[g, x])
            ahead_of = tuple(
                jnp.concatenate([ft[g, x, n], path[g, n]], axis=0) for n in range(2)
            )
            both = mul(ahead_of, split(hom[g, x]))
            hom[g, x + 1] = both[:nv]
            echo[g] += both[nv:]
            omega[g, x + 1] = mul(onward, get(bt, g, x))
            path[g, 0], path[g, 1] = onward
        return carry

    loop(cells, hom_forward, 0, 12)
    for g in range(groups):
        total = echo[g] + mul((path[g, 0], path[g, 1]), split(hom[g, cells]))
        gmap[gx, g * nv : (g + 1) * nv] = jnp.concatenate(
            [total[:, :nv], omega[g, cells]], axis=1
        )
    gmap[gx, groups * nv :] = jnp.concatenate(
        [hom[g, cells][:, :nv] for g in range(groups)], axis=1
    )

    def share(buffer, send, recv, slot, target, k):
        return pltpu.make_async_remote_copy(
            src_ref=buffer.at[slot],
            dst_ref=buffer.at[slot],
            send_sem=send.at[k],
            recv_sem=recv.at[slot],
            device_id=(target, yz),
            device_id_type=MESH,
        )

    def offer(*where):
        for k in range(1, half):
            share(*where, gx, peer(k), k).start()
        share(*where, gx, partner, 0).start()

    def relay(*where):
        for k in range(1, half):
            share(*where, peer(k), peer(k), k).wait_recv()
            share(*where, peer(k), partner, half + k).start()

    def collect(*where):
        share(*where, partner, partner, 0).wait_recv()
        for k in range(1, half):
            share(*where, lax.rem(partner + 2 * k, n_gx), partner, half + k).wait_recv()

    def release(*where):
        share(*where, gx, partner, 0).wait_send()
        for k in range(1, half):
            share(*where, gx, peer(k), k).wait_send()
            share(*where, peer(k), partner, half + k).wait_send()

    maps = (gmap, map_send, map_recv)
    for r in range(1, bits - 1):
        if r > 1:
            hail(ready.at[r])
        pl.semaphore_wait(ready.at[r], bits)
    offer(*maps)

    for g in range(groups):
        tall[g, :nv] = unit
        tall[g, nv:] = jnp.zeros((nv, nv), F32)
        wide_state[g] = second_unit

    def hom_backward(i, carry):
        x = cells - 1 - i
        for g in range(groups):
            m = hom[g, x + 1] + mul(get(bt, g, x), split(wide_state[g]))
            resp[g, 0, x], resp[g, 1, x] = split(m)
            wide_state[g] = m
            now = split(
                jnp.concatenate([tall[g, :nv], omega[g, x] + tall[g, nv:]], axis=0)
            )
            put(gain, g, x, split(mul(now, get(vt, g, x))))
            tall[g] = mul(now, get(ft, g, x))
        return carry

    loop(cells, hom_backward, 0, 4)

    block = next(c for c in (12, 6, 4, 3, 2, 1) if cells % c == 0)

    def weight(g, x):
        kind = cat[x][g : g + 1]
        return jnp.where(kind == 0, 1.0, jnp.where(kind == 2, 0.5, 0.0))

    def slope(g, x):
        if g == 0:
            return 8.0 * res[x, 1] + low[g, x] - high[g, x]
        return low[g, x] + high[g, x] - 8.0 * res[x, 0]

    def arrive(g, c):
        @pl.when(has_low)
        def _():
            halo(0, g, c).wait_recv()

        @pl.when(has_high)
        def _():
            halo(1, g, c).wait_recv()

    def local_forward(g, first, count, gather):
        xs = range(first, first + count)
        flux_in = [mul(held(g, 0), split(slope(g, x))) for x in xs]
        forces = [split(weight(g, x) * (res[x, g] + f)) for x, f in zip(xs, flux_in)]
        if gather:
            total = acc[g]
            for x, force in zip(xs, forces):
                total = total + mul(get(gain, g, x), force)
            acc[g] = total
        for x, force in zip(xs, forces):
            cs[g, x] = mul(get(vt, g, x), force)

    def parcel(g, target):
        return pltpu.make_async_remote_copy(
            src_ref=given.at[g, target],
            dst_ref=taken.at[g, gx],
            send_sem=vec_send.at[g, target],
            recv_sem=vec_recv.at[g, gx],
            device_id=(target, yz),
            device_id_type=MESH,
        )

    def receive(g, source):
        pltpu.make_async_remote_copy(
            src_ref=given.at[g, source],
            dst_ref=taken.at[g, source],
            send_sem=vec_send.at[g, source],
            recv_sem=vec_recv.at[g, source],
            device_id=(source, yz),
            device_id_type=MESH,
        ).wait_recv()

    def compose(g):
        ah, al = split(acc[g])
        for t in range(0, n_gx, 4):
            z = tuple(send_map[g, m, t : t + 4].reshape(4 * nv, 2 * nv) for m in range(2))
            given[g, t : t + 4] = mul(z, (ah, al)).reshape(4, nv, nz)

    def dispatch(g):
        for k in range(1, n_gx):
            parcel(g, lax.rem(gx + k, n_gx)).start()

    def sweep_forward(first, count):
        def forward(i, carry):
            for g in range(groups):
                state = cs[g, i] + mul(get(ft, g, i), split(into_state[g]))
                into_state[g] = state
                cs[g, i] = state
            return carry

        loop(count, lambda i, carry: forward(first + i, carry), 0, 4)

    def sweep_backward():
        for g in range(groups):
            into_state[g] = jnp.zeros((nv, nz), F32)

        def backward(i, carry):
            x = cells - 1 - i
            for g in range(groups):
                state = cs[g, x] + mul(get(bt, g, x), split(into_state[g]))
                into_state[g] = state
                cs[g, x] = state
            return carry

        loop(cells, backward, 0, 4)

    def finish(g):
        head = jnp.zeros((nv, nz), F32)
        tail = given[g, gx]
        for k in range(1, n_gx):
            j = lax.rem(gx + k, n_gx)
            receive(g, j)
            value = taken[g, j]
            head = head + jnp.where(j < gx, value, 0.0)
            tail = tail + jnp.where(j < gx, 0.0, value)
        both = split(jnp.concatenate([head, tail], axis=0))
        high_block = next(c for c in (4, 3, 2, 1) if cells % c == 0)
        for x in range(0, cells, high_block):
            maps_here = tuple(
                resp[g, n, x : x + high_block].reshape(high_block * nv, 2 * nv) for n in range(2)
            )
            fix = mul(maps_here, both).reshape(high_block, nv, nz)
            for k in range(high_block):
                value = cs[g, x + k] + fix[k]
                out[x + k, g] = jnp.where(cat[x + k][g : g + 1] != 1, value, 0.0)

    def turned(g):
        sp = side[g]
        turn = split(
            jnp.concatenate(
                [first_unit, jnp.concatenate([sp, unit], axis=1)], axis=0
            )
        )
        high_block = next(c for c in (4, 3, 2, 1) if cells % c == 0)
        for x in range(0, cells, high_block):
            maps_here = tuple(
                resp[g, n, x : x + high_block].reshape(high_block * nv, 2 * nv) for n in range(2)
            )
            fixed = split(mul(maps_here, turn))
            for n in range(2):
                resp[g, n, x : x + high_block] = fixed[n].reshape(high_block, nv, 2 * nv)

    for g in range(groups):
        acc[g] = jnp.zeros((2 * nv, nz), F32)

    for n in range(chunk):
        x = edge + n
        pair = split(mul(get(gain, last, x), held(last, 0)))
        for m in range(2):
            fast[m, :, n * nv : (n + 1) * nv] = pair[m]
        acc[last] += mul(get(gain, last, x), split(weight(last, x) * res[x, last]))

    relay(*maps)
    for c in every:
        arrive(0, c)
    for x in range(0, cells, block):
        local_forward(0, x, block, True)
    arrive(last, 0)
    local_forward(last, 0, parts[0][1] if pieces > 1 else 0, True)
    collect(*maps)

    for g in range(groups):
        for t in range(2):
            ahead[g, t] = unit
            behind[g, n_gx - t] = unit
            mirror[g, t] = unit

    def chains(n, carry):
        t = n + 1
        i = n_gx - 1 - t
        p_up = gmap[t, groups * nv :]
        grow = t > gx
        shrink = i < gx
        for g in range(groups):
            rows = slice(g * nv, (g + 1) * nv)
            step = mul(split(p_up[:, rows]), split(ahead[g, t]))
            ahead[g, t + 1] = jnp.where(grow, step, unit)
            step = mul(split(gmap[i, rows][:, nv:]), split(behind[g, i + 1]))
            behind[g, i] = jnp.where(shrink, step, unit)
            step = mul(split(mirror[g, t]), split(gmap[t, rows][:, nv:]))
            mirror[g, t + 1] = jnp.where(grow, step, unit)
        return carry

    loop(n_gx - 2, chains, 0, 6)

    for g in range(groups):
        rows = slice(g * nv, (g + 1) * nv)
        s_now = jnp.zeros((nv, nv), F32)
        inner = [mul(split(gmap[j, rows][:, :nv]), split(ahead[g, j])) for j in range(1, n_gx)]
        for j in range(1, n_gx):
            s_now = s_now + jnp.where(j > gx, mul(split(mirror[g, j]), split(inner[j - 1])), 0.0)
        zero = jnp.zeros((nv, nv), F32)
        qs = mul(split(gmap[gx, rows][:, nv:]), split(s_now))
        p_here = gmap[gx, groups * nv :][:, rows]
        sp = mul(split(s_now), split(p_here))
        left = jnp.concatenate([qs, unit], axis=1)
        for i in range(n_gx):
            m = mul(split(behind[g, i + 1]), split(left))
            m = jnp.where(i < gx, m, jnp.concatenate([ahead[g, i], zero], axis=1))
            m = jnp.where(gx == i, jnp.concatenate([s_now, zero], axis=1), m)
            send_map[g, 0, i], send_map[g, 1, i] = split(m)
        side[g] = sp

    compose(0)
    dispatch(0)

    for t in range(0, n_gx, 4):
        z = tuple(send_map[last, m, t : t + 4].reshape(4 * nv, 2 * nv) for m in range(2))
        quick = split(mul(z, (fast[0], fast[1])))
        for m in range(2):
            zfast[m, t : t + 4] = quick[m].reshape(4, nv, chunk * nv)
    for g in range(groups):
        turned(g)
    for g in range(groups):
        into_state[g] = jnp.zeros((nv, nz), F32)

    done = 0
    for c in every[1:-1]:
        arrive(last, c)
        local_forward(last, *parts[c], True)
        if c < pieces - 2 and True:
            sweep_forward(done, sum(parts[c]) - done)
            done = sum(parts[c])
    compose(last)

    arrive(last, pieces - 1)
    late = split(
        jnp.concatenate(
            [weight(last, x) * slope(last, x) for x in range(edge, cells)], axis=0
        )
    )
    for t in range(0, n_gx, 4):
        z = tuple(zfast[m, t : t + 4].reshape(4 * nv, chunk * nv) for m in range(2))
        given[last, t : t + 4] += mul(z, late).reshape(4, nv, nz)
    dispatch(last)
    local_forward(last, edge, chunk, False)

    sweep_forward(done, cells - done)
    sweep_backward()
    for g in range(groups):
        finish(g)

    @pl.when(has_high)
    def _():
        for g in range(groups):
            for c in range(pieces):
                halo(0, g, c).wait_send()

    @pl.when(has_low)
    def _():
        for g in range(groups):
            for c in range(pieces):
                halo(1, g, c).wait_send()

    release(*maps)
    for g in range(groups):
        for k in range(1, n_gx):
            parcel(g, lax.rem(gx + k, n_gx)).wait_send()


def per_device(n_gx, n_yz, residual, inverses, upwind, downwind, flux_y, kinds, volume_category):
    cells, groups, nv, nz = residual.shape
    pieces = len(cuts(cells))
    chunk = cuts(cells)[-1][1]
    hbm = pl.BlockSpec(memory_space=pltpu.HBM)
    operands = (residual, inverses, upwind, downwind, flux_y, volume_category, kinds)
    square = pltpu.VMEM((groups, cells, 2, nv, nv), BF16)
    wide = pltpu.VMEM((groups, cells, nv, nz), F32)
    return pl.pallas_call(
        functools.partial(kernel, n_gx, n_yz),
        out_shape=jax.ShapeDtypeStruct(residual.shape, F32),
        in_specs=[hbm] * 7,
        out_specs=pl.BlockSpec(memory_space=pltpu.VMEM),
        scratch_shapes=[pltpu.VMEM(a.shape, a.dtype) for a in operands[:-1]]
        + [
            pltpu.SMEM(kinds.shape, kinds.dtype),
            pltpu.VMEM((2, cells, nv, nz), F32),
            wide,
            wide,
            pltpu.VMEM((groups, 3, 2, nv, nv), BF16),
            square,
            square,
            square,
            pltpu.VMEM((groups, max(cells, n_gx) + 1, nv, 2 * nv), F32),
            pltpu.VMEM((groups, cells + 1, nv, nv), F32),
            pltpu.VMEM((groups, 2, nv, nv), BF16),
            pltpu.VMEM((groups, nv, 2 * nv), F32),
            pltpu.VMEM((groups, cells, 2, 2 * nv, nv), BF16),
            pltpu.VMEM((2, 2 * nv, chunk * nv), BF16),
            pltpu.VMEM((2, n_gx, nv, chunk * nv), BF16),
            pltpu.VMEM((groups, 2, cells, nv, 2 * nv), BF16),
            wide,
            pltpu.VMEM((groups, 2 * nv, nz), F32),
            pltpu.VMEM((n_gx, (groups + 1) * nv, 2 * nv), F32),
            pltpu.VMEM((groups, n_gx, nv, nz), F32),
            pltpu.VMEM((groups, n_gx, nv, nz), F32),
            pltpu.VMEM((groups, 2, n_gx, nv, 2 * nv), BF16),
            pltpu.VMEM((groups, n_gx + 1, nv, nv), F32),
            pltpu.VMEM((groups, n_gx + 1, nv, nv), F32),
            pltpu.VMEM((groups, n_gx + 1, nv, nv), F32),
            pltpu.VMEM((groups, nv, nv), F32),
            pltpu.VMEM((groups, nv, 2 * nv), F32),
            pltpu.VMEM((groups, 2 * nv, nv), F32),
            pltpu.VMEM((groups, nv, nz), F32),
            pltpu.SemaphoreType.DMA((7,)),
            pltpu.SemaphoreType.DMA((2, groups, pieces)),
            pltpu.SemaphoreType.DMA((2, groups, pieces)),
            pltpu.SemaphoreType.DMA((n_gx,)),
            pltpu.SemaphoreType.DMA((n_gx,)),
            pltpu.SemaphoreType.DMA((groups, n_gx)),
            pltpu.SemaphoreType.DMA((groups, n_gx)),
            pltpu.SemaphoreType.REGULAR((max(n_gx.bit_length() - 2, 1),)),
        ],
        compiler_params=pltpu.CompilerParams(
            collective_id=0, has_side_effects=True, vmem_limit_bytes=48 * 1024 * 1024
        ),
    )(*(pltpu.with_memory_space_constraint(a, pltpu.HBM) for a in operands))


def solution(mesh):
    in_specs = (
        P("gx", "yz", None, None),
        P("gx", "yz", None, None),
        P(),
        P(),
        P(),
        P("yz"),
        P("gx", "yz", None),
    )
    out_specs = P("gx", "yz", None, None)
    return jax.shard_map(
        functools.partial(per_device, mesh.shape["gx"], mesh.shape["yz"]),
        mesh=mesh,
        in_specs=in_specs,
        out_specs=out_specs,
        check_vma=False,
    )
```
